32 devices in a mesh: shard: 8 (over z, x), head: 4 (over y, core).
Axes of the slice: x: 2, y: 2, z: 4, core: 2. Of those that a mesh axis runs over, the one named last changes fastest.
Arguments:
- resid_in: float32 [2048, 1024], P(('shard', 'head')), may hold values from -6 to 6
- cotangent: float32 [2048, 1024], P(('shard', 'head')), may hold values from -6 to 6
- segment: int32 [2048], P('shard'), may hold values from 0 to 3, never falling along the last dimension, each value on 1 to 1024 neighbouring positions
- attn_gain: bfloat16 [1024], P('shard'), may hold values from 0.25 to 1.75
- w_query: bfloat16 [1024, 512], P('shard', 'head'), may hold values from -0.1875 to 0.1875
- w_key: bfloat16 [1024, 512], P('shard', 'head'), may hold values from -0.1875 to 0.1875
- w_value: bfloat16 [1024, 1024], P('shard', 'head'), may hold values from -0.1875 to 0.1875
- w_outgate: bfloat16 [1024, 1024], P('shard', 'head'), may hold values from -0.1875 to 0.1875
- w_low: bfloat16 [1024, 16], P('shard'), may hold values from -0.1875 to 0.1875
- w_rank: bfloat16 [16, 4, 128], P(None, 'head', 'shard'), may hold values from -1.5 to 1.5
- rank_bias: bfloat16 [4, 128], P('head', 'shard'), may hold values from -3 to 9
- head_gain: bfloat16 [256], P('shard'), may hold values from 0.25 to 1.75
- w_out: bfloat16 [1024, 1024], P('head', 'shard'), may hold values from -0.1875 to 0.1875
- mlp_gain: bfloat16 [1024], P('shard'), may hold values from 0.25 to 1.75
- w_gate: bfloat16 [1024, 2816], P('shard', 'head'), may hold values from -0.1875 to 0.1875
- w_up: bfloat16 [1024, 2816], P('shard', 'head'), may hold values from -0.1875 to 0.1875
- w_down: bfloat16 [2816, 1024], P('head', 'shard'), may hold values from -0.109375 to 0.109375
Outputs:
- resid_out: float32 [2048, 1024], P(('shard', 'head'))
- grad_in: float32 [2048, 1024], P(('shard', 'head'))
- grad_attn_gain: float32 [1024], P(('shard', 'head'))
- grad_w_query: float32 [1024, 512], P('shard', 'head')
- grad_w_key: float32 [1024, 512], P('shard', 'head')
- grad_w_value: float32 [1024, 1024], P('shard', 'head')
- grad_w_outgate: float32 [1024, 1024], P('shard', 'head')
- grad_w_low: float32 [1024, 16], P(('shard', 'head'))
- grad_w_rank: float32 [16, 4, 128], P(None, 'head', 'shard')
- grad_rank_bias: float32 [4, 128], P('head', 'shard')
- grad_head_gain: float32 [256], P(('shard', 'head'))
- grad_w_out: float32 [1024, 1024], P('head', 'shard')
- grad_mlp_gain: float32 [1024], P(('shard', 'head'))
- grad_w_gate: float32 [1024, 2816], P('shard', 'head')
- grad_w_up: float32 [1024, 2816], P('shard', 'head')
- grad_w_down: float32 [2816, 1024], P('head', 'shard')
The draws below stay inside these ranges and needn't reach their ends.
Inputs may be any that keep to these rules, and one draw needn't show every extreme that they name: `segment`: document ids never fall along the token stream; each id covers 1 to 1024 consecutive tokens and some id covers exactly 1024.
All inputs are finite; a program needn't handle non-finite values.
Results may differ from the reference program's by a relative error of at most 0.019.
Values may be sent and summed in bfloat16 or wider, within the bound.
A program may use at most 128 MiB of HBM per device.

```python
import math
import jax
import jax.numpy as jnp
import numpy as np
from jax import lax

D = 1024
HEADS = 4
DK = 128
DV = 256
GATE_RANK = 16
FF = 2816
GROUP = 64
SEQ = 1024
TOKENS = 2048


def raised(values, key, source, target, parts, factor):
    def block_of(position):
        return (jnp.arange(values.shape[position]) // (values.shape[position] // parts)).reshape((-1,) + (1,) * (values.ndim - 1 - position))

    first = jax.random.permutation(key, parts)[block_of(target)]
    far = (block_of(target) + parts // 2) % parts
    return jnp.where((block_of(source) == first) | (block_of(source) == far), factor * values, values)


def steps_of(key, shape, cuts, low, top_value):
    def one(axis_at, shards_of):
        draws = jax.random.uniform(jax.random.fold_in(jax.random.fold_in(key, 6), axis_at), (shards_of,), jnp.float32, low / len(cuts), top_value / len(cuts))
        return jnp.repeat(jnp.exp(draws), shape[axis_at] // shards_of).reshape((-1,) + (1,) * (len(shape) - axis_at - 1))

    factor_of = one(*cuts[0])
    for cut in cuts[1:]:
        factor_of = factor_of * one(*cut)
    return factor_of


def length_profile(number_of, total, most, slope):
    portions = [(1 << 20) // math.isqrt(standing ** slope) + 1 for standing in range(2, number_of + 1)]
    surplus, given = total - most - (number_of - 1), [1] * (number_of - 1)
    while surplus > 0:
        candidates = [i for i in range(number_of - 1) if given[i] < most]
        whole, left = sum([portions[i] for i in candidates]), surplus
        for i in candidates:
            addition = min(most - given[i], max(1, left * portions[i] // whole), surplus)
            given[i] = given[i] + addition
            surplus = surplus - addition
    return np.array([most] + given)


def ragged(rng, amount, total, most, slope):
    if amount == 2:
        one = jax.random.randint(rng, (), max(1, total - most), min(most, total - 1) + 1)
        return jnp.stack([one, total - one])
    tallies = jnp.asarray(length_profile(amount, total, most, slope), jnp.int32)
    couples = (amount - 1) // 2
    giver, sink = tallies[1:1 + 2 * couples:2], tallies[2:2 + 2 * couples:2]
    room = jnp.minimum(giver - 1, most - sink)
    moved = jax.random.randint(jax.random.fold_in(rng, 1), (couples,), 0, 1 << 20) % (room + 1)
    tallies = tallies.at[1:1 + 2 * couples:2].set(giver - moved).at[2:2 + 2 * couples:2].set(sink + moved)
    return tallies[jax.random.permutation(jax.random.fold_in(rng, 2), amount)]


def noise(own_key, extent, deviation, bound, cuts=(), held_as=jnp.bfloat16):
    values = deviation * jax.random.normal(own_key, extent, jnp.float32)
    if cuts:
        values = values * steps_of(own_key, extent, cuts, -0.22, 0.18)
    return jnp.clip(values, -bound, bound).astype(held_as)


def noise_with(own_key, dims, deviation, most, shards, heavy, held_as=jnp.bfloat16):
    entries = deviation * jax.random.normal(own_key, dims, jnp.float32)
    if shards:
        entries = entries * steps_of(own_key, dims, shards, -0.22, 0.18)
    return jnp.clip(raised(entries, jax.random.fold_in(own_key, 3), *heavy), -most, most).astype(held_as)


def setup_inputs(seed: int = 0) -> dict:
    streams_of = jax.random.split(jax.random.key(seed), 18)
    resid_in = noise(streams_of[0], (TOKENS, D), 1.0, 6.0, ((0, 32),), jnp.float32)
    cotangent = noise_with(streams_of[1], (TOKENS, D), 1.0, 6.0, ((0, 32),), (0, 1, 32, 2.75), jnp.float32)
    segment = jnp.searchsorted(jnp.cumsum(ragged(streams_of[2], 2 * TOKENS // SEQ, TOKENS, SEQ, 1)), jnp.arange(TOKENS), side="right").astype(jnp.int32)
    attn_gain = jnp.clip(1.0 + 0.15 * jax.random.normal(streams_of[3], (D,), jnp.float32), 0.25, 1.75).astype(jnp.bfloat16)
    w_query = noise(streams_of[4], (D, HEADS * DK), D ** -0.5, 0.1875, ((0, 8), (1, 4)))
    w_key = noise(streams_of[5], (D, HEADS * DK), D ** -0.5, 0.1875, ((0, 8), (1, 4)))
    w_value = noise(streams_of[6], (D, HEADS * DV), D ** -0.5, 0.1875, ((0, 8), (1, 4)))
    w_outgate = noise(streams_of[7], (D, HEADS * DV), D ** -0.5, 0.1875, ((0, 8), (1, 4)))
    w_low = noise(streams_of[8], (D, GATE_RANK), D ** -0.5, 0.1875, ((0, 8),))
    w_rank = noise(streams_of[9], (GATE_RANK, HEADS, DK), GATE_RANK ** -0.5, 1.5, ((1, 4), (2, 8)))
    rank_bias = jnp.clip(-3.0 + 12.0 * jax.random.uniform(streams_of[10], (HEADS, DK), jnp.float32) ** steps_of(streams_of[10], (HEADS, DK), ((0, 4), (1, 8)), -0.2, 0.2), -3.0, 9.0).astype(jnp.bfloat16)
    head_gain = jnp.clip(1.0 + 0.15 * jax.random.normal(streams_of[11], (DV,), jnp.float32), 0.25, 1.75).astype(jnp.bfloat16)
    w_out = noise(streams_of[12], (HEADS * DV, D), (HEADS * DV) ** -0.5, 0.1875, ((0, 4), (1, 8)))
    mlp_gain = jnp.clip(1.0 + 0.15 * jax.random.normal(streams_of[13], (D,), jnp.float32), 0.25, 1.75).astype(jnp.bfloat16)
    w_gate = noise(streams_of[14], (D, FF), D ** -0.5, 0.1875, ((0, 8), (1, 4)))
    w_up = noise(streams_of[15], (D, FF), D ** -0.5, 0.1875, ((0, 8), (1, 4)))
    w_down = noise(streams_of[16], (FF, D), FF ** -0.5, 0.109375, ((0, 4), (1, 8)))
    return dict(resid_in=resid_in, cotangent=cotangent, segment=segment, attn_gain=attn_gain, w_query=w_query, w_key=w_key, w_value=w_value, w_outgate=w_outgate, w_low=w_low, w_rank=w_rank, rank_bias=rank_bias, head_gain=head_gain, w_out=w_out, mlp_gain=mlp_gain, w_gate=w_gate, w_up=w_up, w_down=w_down)


EPS = 1e-06
HIGH_PRECISION = lax.Precision.HIGHEST

def rms_scale(values):
    return lax.rsqrt(lax.optimization_barrier(jnp.mean(values * values, axis=-1, keepdims=True)) + EPS)

def group_pass(query, key, value_rows, logdec, segf, state, carry_seg):
    total = query.shape[0]
    heads = query.shape[1]
    count = total // GROUP
    scale = DK ** (-0.5)
    order = jnp.arange(GROUP)
    causal = order[:, None] >= order[None, :]

    def blocks(array):
        return array.reshape((count, GROUP) + array.shape[1:])

    def advance(carry, pieces):
        memory_state, prior = carry
        query_c, key_c, value_segment, decay_c, seg_c = pieces
        cumul = jnp.cumsum(decay_c, axis=0)
        query_decayed = query_c * jnp.exp(cumul) * scale
        key_inc = key_c * jnp.exp(-cumul)
        scores = jnp.einsum('thk,shk->hts', query_decayed, key_inc, precision=HIGH_PRECISION)
        joined = jnp.logical_and(causal, seg_c[:, None] == seg_c[None, :])
        scores = jnp.where(joined[None], scores, 0.0)
        inherit = (seg_c == prior).astype(jnp.float32)
        inside = jnp.einsum('hts,shv->thv', scores, value_segment, precision=HIGH_PRECISION)
        carried_state = jnp.einsum('zsb,sbi->zsi', query_decayed, memory_state, precision=HIGH_PRECISION)
        result = inside + inherit[:, None, None] * carried_state
        final_result = cumul[-1]
        keep = (seg_c == seg_c[-1]).astype(jnp.float32)
        key_final_rows = key_c * jnp.exp(final_result[None] - cumul) * keep[:, None, None]
        linked_states = (seg_c[-1] == prior).astype(jnp.float32)
        memory_state = linked_states * jnp.exp(final_result)[:, :, None] * memory_state + jnp.einsum('zie,zir->ier', key_final_rows, value_segment, precision=HIGH_PRECISION)
        return ((memory_state, seg_c[-1]), result)
    (memory_state, last_seg), outs = lax.scan(advance, (state, carry_seg), (blocks(query), blocks(key), blocks(value_rows), blocks(logdec), blocks(segf)))
    return (outs.reshape(total, heads, outs.shape[-1]), memory_state)

def reference(resid_in, cotangent, segment, attn_gain, w_query, w_key, w_value, w_outgate, w_low, w_rank, rank_bias, head_gain, w_out, mlp_gain, w_gate, w_up, w_down):
    total = resid_in.shape[0]
    gain_attn = attn_gain.astype(jnp.float32)
    inv_attn = rms_scale(resid_in)
    normed_in = (resid_in * inv_attn * gain_attn).astype(jnp.bfloat16)
    query = jnp.dot(normed_in, w_query, preferred_element_type=jnp.float32).reshape(total, HEADS, DK)
    key = jnp.dot(normed_in, w_key, preferred_element_type=jnp.float32).reshape(total, HEADS, DK)
    value_rows = jnp.dot(normed_in, w_value, preferred_element_type=jnp.float32).reshape(total, HEADS, DV)
    outgate = jnp.dot(normed_in, w_outgate, preferred_element_type=jnp.float32).reshape(total, HEADS, DV)
    low = jnp.dot(normed_in, w_low, preferred_element_type=jnp.float32)
    rank_mat = w_rank.astype(jnp.float32).reshape(GATE_RANK, HEADS * DK)
    logit = jnp.dot(low, rank_mat, precision=HIGH_PRECISION) + rank_bias.astype(jnp.float32).reshape(HEADS * DK)
    logdec = (jax.nn.log_sigmoid(logit) / 16.0).reshape(total, HEADS, DK)
    segf = segment.astype(jnp.float32) + 1.0
    start_state = jnp.zeros((HEADS, DK, DV), jnp.float32)
    start_seg = jnp.zeros((), jnp.float32)

    def mixer(query_in, key_in, value_in, decay_in):
        return group_pass(query_in, key_in, value_in, decay_in, segf, start_state, start_seg)[0]
    mixed, mixer_back = jax.vjp(mixer, query, key, value_rows, logdec)
    inv_head = rms_scale(mixed)
    gain_head = head_gain.astype(jnp.float32)
    headnormed = mixed * inv_head * gain_head
    sigma_out = jax.nn.sigmoid(outgate)
    swish_out = outgate * sigma_out
    gated = (headnormed * swish_out).reshape(total, HEADS * DV).astype(jnp.bfloat16)
    resid_mid = resid_in + jnp.dot(gated, w_out, preferred_element_type=jnp.float32)
    width = math.gcd(total, 4096)
    nblocks = total // width
    gain_mlp = mlp_gain.astype(jnp.float32)

    def mlp_step(sums, rows):
        resid, cot = rows
        inv_mlp = rms_scale(resid)
        normed_mid = (resid * inv_mlp * gain_mlp).astype(jnp.bfloat16)
        gate_pre = jnp.dot(normed_mid, w_gate, preferred_element_type=jnp.float32)
        up_pre = jnp.dot(normed_mid, w_up, preferred_element_type=jnp.float32)
        sigma_gate = jax.nn.sigmoid(gate_pre)
        active = gate_pre * sigma_gate
        hidden = (active * up_pre).astype(jnp.bfloat16)
        result = resid + jnp.dot(hidden, w_down, preferred_element_type=jnp.float32)
        cot_bf = cot.astype(jnp.bfloat16)
        d_hidden = jnp.dot(cot_bf, w_down.T, preferred_element_type=jnp.float32)
        d_gatepre = (d_hidden * up_pre * sigma_gate * (1.0 + gate_pre * (1.0 - sigma_gate))).astype(jnp.bfloat16)
        d_uppre = (d_hidden * active).astype(jnp.bfloat16)
        grad_down = sums[0] + jnp.dot(hidden.T, cot_bf, preferred_element_type=jnp.float32)
        grad_gate = sums[1] + jnp.dot(normed_mid.T, d_gatepre, preferred_element_type=jnp.float32)
        grad_up = sums[2] + jnp.dot(normed_mid.T, d_uppre, preferred_element_type=jnp.float32)
        d_normmid = jnp.dot(d_gatepre, w_gate.T, preferred_element_type=jnp.float32) + jnp.dot(d_uppre, w_up.T, preferred_element_type=jnp.float32)
        grad_gain = sums[3] + lax.optimization_barrier(jnp.sum(d_normmid * resid * inv_mlp, axis=0))
        scaled = gain_mlp * d_normmid
        d_resid = cot + inv_mlp * scaled - resid * inv_mlp ** 3 * lax.optimization_barrier(jnp.mean(scaled * resid, axis=-1, keepdims=True))
        return ((grad_down, grad_gate, grad_up, grad_gain), (result, d_resid))
    start_sums = (jnp.zeros((FF, D), jnp.float32), jnp.zeros((D, FF), jnp.float32), jnp.zeros((D, FF), jnp.float32), jnp.zeros((D,), jnp.float32))
    sums, outs = lax.scan(mlp_step, start_sums, (resid_mid.reshape(nblocks, width, D), cotangent.reshape(nblocks, width, D)))
    grad_w_down, grad_w_gate, grad_w_up, grad_mlp_gain = sums
    resid_out = outs[0].reshape(total, D)
    d_mid = outs[1].reshape(total, D)
    dmid_bf = d_mid.astype(jnp.bfloat16)
    d_gated = jnp.dot(dmid_bf, w_out.T, preferred_element_type=jnp.float32).reshape(total, HEADS, DV)
    grad_w_out = jnp.dot(gated.T, dmid_bf, preferred_element_type=jnp.float32)
    d_head = d_gated * swish_out
    d_outgate = (d_gated * headnormed * sigma_out * (1.0 + outgate * (1.0 - sigma_out))).reshape(total, HEADS * DV).astype(jnp.bfloat16)
    grad_head_gain = lax.optimization_barrier(jnp.sum(d_head * mixed * inv_head, axis=(0, 1)))
    scaled_head = gain_head * d_head
    mixed_gradient = inv_head * scaled_head - mixed * inv_head ** 3 * lax.optimization_barrier(jnp.mean(scaled_head * mixed, axis=-1, keepdims=True))
    d_query, d_key, d_value, d_logdec = mixer_back(mixed_gradient)
    query_bf = d_query.reshape(total, HEADS * DK).astype(jnp.bfloat16)
    key_bf = d_key.reshape(total, HEADS * DK).astype(jnp.bfloat16)
    value_bf = d_value.reshape(total, HEADS * DV).astype(jnp.bfloat16)
    d_logit = d_logdec.reshape(total, HEADS * DK) * jax.nn.sigmoid(-logit) / 16.0
    grad_rank_bias = lax.optimization_barrier(jnp.sum(d_logit, axis=0)).reshape(HEADS, DK)
    grad_w_rank = jnp.dot(low.T, d_logit, precision=HIGH_PRECISION).reshape(GATE_RANK, HEADS, DK)
    d_low = jnp.einsum('thk,rhk->thr', d_logit.reshape(total, HEADS, DK), w_rank.astype(jnp.float32), precision=HIGH_PRECISION).astype(jnp.bfloat16).reshape(total, HEADS * GATE_RANK)
    grad_w_low = jnp.dot(normed_in.T, d_low, preferred_element_type=jnp.float32).reshape(D, HEADS, GATE_RANK).sum(axis=1)
    grad_w_query = jnp.dot(normed_in.T, query_bf, preferred_element_type=jnp.float32)
    grad_w_key = jnp.dot(normed_in.T, key_bf, preferred_element_type=jnp.float32)
    grad_w_value = jnp.dot(normed_in.T, value_bf, preferred_element_type=jnp.float32)
    grad_w_outgate = jnp.dot(normed_in.T, d_outgate, preferred_element_type=jnp.float32)
    low_rows = jnp.tile(w_low.T, (HEADS, 1))
    d_normin = jnp.dot(query_bf, w_query.T, preferred_element_type=jnp.float32)
    d_normin = d_normin + jnp.dot(key_bf, w_key.T, preferred_element_type=jnp.float32)
    d_normin = d_normin + jnp.dot(value_bf, w_value.T, preferred_element_type=jnp.float32)
    d_normin = d_normin + jnp.dot(d_outgate, w_outgate.T, preferred_element_type=jnp.float32)
    d_normin = d_normin + jnp.dot(d_low, low_rows, preferred_element_type=jnp.float32)
    grad_attn_gain = lax.optimization_barrier(jnp.sum(d_normin * resid_in * inv_attn, axis=0))
    scaled_in = gain_attn * d_normin
    grad_in = d_mid + inv_attn * scaled_in - resid_in * inv_attn ** 3 * lax.optimization_barrier(jnp.mean(scaled_in * resid_in, axis=-1, keepdims=True))
    return (resid_out, grad_in, grad_attn_gain, grad_w_query, grad_w_key, grad_w_value, grad_w_outgate, grad_w_low, grad_w_rank, grad_rank_bias, grad_head_gain, grad_w_out, grad_mlp_gain, grad_w_gate, grad_w_up, grad_w_down)
```

```python
import functools

import jax
import jax.numpy as jnp
from jax import lax
from jax.experimental import pallas as pl
from jax.experimental.pallas import tpu as pltpu
from jax.sharding import PartitionSpec as P

D = 1024
DK = 128
DV = 256
GATE_RANK = 16
GROUP = 64
LANE = 128
SHARD = "shard"
HEAD = "head"
MESH = pl.DeviceIdType.MESH


EPS = 1e-06
HIGH_PRECISION = lax.Precision.HIGHEST


def ring_index(pos, n):
    return jnp.where(pos < n // 2, 2 * pos, 2 * (n - 1 - pos) + 1)


def ring_place(index, n):
    return jnp.where(index % 2 == 0, index // 2, n - 1 - index // 2)


def greet(*pairs):
    barrier = pltpu.get_barrier_semaphore()
    for axis, peer in pairs:
        pl.semaphore_signal(barrier, inc=1, device_id={axis: peer}, device_id_type=MESH)
    pl.semaphore_wait(barrier, len(pairs))


def remote(source, target, send_sem, recv_sem, axis, peer):
    return pltpu.make_async_remote_copy(
        src_ref=source,
        dst_ref=target,
        send_sem=send_sem,
        recv_sem=recv_sem,
        device_id={axis: peer},
        device_id_type=MESH,
    )


def quad(axis):
    me = lax.axis_index(axis)
    return me, me + 1 - 2 * (me % 2), (me + 2) % 4


def cuts(columns, parts):
    lanes = columns // LANE
    sizes = [(lanes // parts + (1 if i < lanes % parts else 0)) * LANE for i in range(parts)]
    starts = [sum(sizes[:i]) for i in range(parts)]
    return list(zip(starts, sizes))


def ring_gather_kernel(n, axis, x_ref, o_ref, own_sem, send_sem, recv_sem):
    right, left = ring_sides(n, axis)
    greet((axis, left), (axis, right))
    ring_gather_body(n, axis, x_ref, o_ref, own_sem, send_sem, recv_sem, None)


def ring_sides(n, axis):
    pos = ring_place(lax.axis_index(axis), n)
    return ring_index((pos + 1) % n, n), ring_index((pos + n - 1) % n, n)


def ring_gather_body(n, axis, x_ref, o_ref, own_sem, send_sem, recv_sem, meanwhile):
    me = lax.axis_index(axis)
    pos = ring_place(me, n)
    right, left = ring_sides(n, axis)
    own = pltpu.make_async_copy(x_ref, o_ref.at[me], own_sem)
    own.start()
    pieces = cuts(x_ref.shape[1], 2)
    steps = n // 2
    sent = {}
    for step in range(steps):
        for part, (start, size) in enumerate(pieces):
            for way in range(2):
                if step == steps - 1 and part != way:
                    continue
                shift = n - step if way == 0 else step
                block = ring_index((pos + shift) % n, n)
                columns = pl.ds(start, size)
                if step > 0:
                    sent[(step - 1, part, way)].wait_recv()
                source = x_ref.at[:, columns] if step == 0 else o_ref.at[block, :, columns]
                copy = pltpu.make_async_remote_copy(
                    src_ref=source,
                    dst_ref=o_ref.at[block, :, columns],
                    send_sem=send_sem.at[step, part, way],
                    recv_sem=recv_sem.at[step, part, way],
                    device_id={axis: right if way == 0 else left},
                    device_id_type=MESH,
                )
                copy.start()
                sent[(step, part, way)] = copy
        if step == 0 and meanwhile is not None:
            meanwhile()
    for (step, part, way), copy in sent.items():
        if (step + 1, part, way) not in sent:
            copy.wait_recv()
    for copy in sent.values():
        copy.wait_send()
    own.wait()


def ring_gather(x, axis, ident):
    n = lax.axis_size(axis)
    return pl.pallas_call(
        functools.partial(ring_gather_kernel, n, axis),
        out_shape=jax.ShapeDtypeStruct((n,) + x.shape, x.dtype),
        in_specs=[pl.BlockSpec(memory_space=pltpu.VMEM)],
        out_specs=pl.BlockSpec(memory_space=pl.ANY),
        scratch_shapes=[
            pltpu.SemaphoreType.DMA,
            pltpu.SemaphoreType.DMA((n // 2, 2, 2)),
            pltpu.SemaphoreType.DMA((n // 2, 2, 2)),
        ],
        compiler_params=pltpu.CompilerParams(collective_id=ident, has_side_effects=True),
    )(x)


def quad_gather_parts(axis, x_ref, o_ref, send_sem, recv_sem):
    me, beside, across = quad(axis)
    half = x_ref.shape[0] // 2
    parts = [pl.ds(0, half), pl.ds(half, half)]
    first = [
        (
            remote(x_ref.at[rows], o_ref.at[me, rows], send_sem.at[i, 0], recv_sem.at[i, 0], axis, across),
            remote(x_ref.at[rows], o_ref.at[me, rows], send_sem.at[i, 1], recv_sem.at[i, 1], axis, beside),
        )
        for i, rows in enumerate(parts)
    ]
    onward = [
        remote(
            o_ref.at[across, rows],
            o_ref.at[across, rows],
            send_sem.at[i, 2],
            recv_sem.at[i, 2],
            axis,
            beside,
        )
        for i, rows in enumerate(parts)
    ]

    def start():
        for far, near in first:
            far.start()
            near.start()
        o_ref[me] = x_ref[...]

    def relay():
        for (far, _), more in zip(first, onward):
            far.wait_recv()
            more.start()

    def finish():
        for (far, near), more in zip(first, onward):
            near.wait_recv()
            more.wait_recv()
            far.wait_send()
            near.wait_send()
            more.wait_send()

    return start, relay, finish


def gather_kernel(axis, x_ref, o_ref, send_sem, recv_sem):
    _, beside, across = quad(axis)
    greet((axis, beside), (axis, across))
    start, relay, finish = quad_gather_parts(axis, x_ref, o_ref, send_sem, recv_sem)
    start()
    relay()
    finish()


def gather(x, axis, ident):
    return pl.pallas_call(
        functools.partial(gather_kernel, axis),
        out_shape=jax.ShapeDtypeStruct((4,) + x.shape, x.dtype),
        in_specs=[pl.BlockSpec(memory_space=pltpu.VMEM)],
        out_specs=pl.BlockSpec(memory_space=pltpu.VMEM),
        scratch_shapes=[
            pltpu.SemaphoreType.DMA((2, 3)),
            pltpu.SemaphoreType.DMA((2, 3)),
        ],
        compiler_params=pltpu.CompilerParams(collective_id=ident, has_side_effects=True),
    )(x)


def enter_kernel(n, w_ref, x_ref, spread_ref, o_ref, own_sem, send_w, recv_w, send_x, recv_x):
    right, left = ring_sides(n, SHARD)
    _, beside, across = quad(HEAD)
    greet((SHARD, left), (SHARD, right), (HEAD, beside), (HEAD, across))
    start, relay, finish = quad_gather_parts(HEAD, x_ref, o_ref, send_x, recv_x)
    start()
    ring_gather_body(n, SHARD, w_ref, spread_ref, own_sem, send_w, recv_w, relay)
    finish()


def enter(weights, x, ident):
    n = lax.axis_size(SHARD)
    return pl.pallas_call(
        functools.partial(enter_kernel, n),
        out_shape=(
            jax.ShapeDtypeStruct((n,) + weights.shape, weights.dtype),
            jax.ShapeDtypeStruct((4,) + x.shape, x.dtype),
        ),
        in_specs=[pl.BlockSpec(memory_space=pltpu.VMEM)] * 2,
        out_specs=(
            pl.BlockSpec(memory_space=pl.ANY),
            pl.BlockSpec(memory_space=pltpu.VMEM),
        ),
        scratch_shapes=[
            pltpu.SemaphoreType.DMA,
            pltpu.SemaphoreType.DMA((n // 2, 2, 2)),
            pltpu.SemaphoreType.DMA((n // 2, 2, 2)),
            pltpu.SemaphoreType.DMA((2, 3)),
            pltpu.SemaphoreType.DMA((2, 3)),
        ],
        compiler_params=pltpu.CompilerParams(collective_id=ident, has_side_effects=True),
    )(weights, x)


def ring_sum_kernel(n, axis, pieces, count, *refs):
    g_refs, o_refs = refs[:count], refs[count : 2 * count]
    held, send_sem, recv_sem = refs[2 * count :]
    me = lax.axis_index(axis)
    pos = ring_place(me, n)
    right, left = ring_sides(n, axis)
    greet((axis, left), (axis, right))

    def slot_of(step, part):
        start, size = pieces[part][3:]
        return held.at[step, :, pl.ds(start, size)]

    def copy_of(step, part, source):
        return remote(
            source,
            slot_of(step, part),
            send_sem.at[step, part],
            recv_sem.at[step, part],
            axis,
            right if pieces[part][1] == 0 else left,
        )

    def own_of(step, part):
        which, way, start, _, size = pieces[part]
        shift = 2 * n - 1 - step if way == 0 else 1 + step
        return g_refs[which].at[ring_index((pos + shift) % n, n), :, pl.ds(start, size)]

    for part in range(len(pieces)):
        copy_of(0, part, own_of(0, part)).start()

    def one(step, carry):
        for part in range(len(pieces)):
            slot = slot_of(step - 1, part)
            copy_of(step - 1, part, slot).wait_recv()
            slot[...] = (
                slot[...].astype(jnp.float32) + own_of(step, part)[...].astype(jnp.float32)
            ).astype(held.dtype)
            copy_of(step, part, slot).start()
        return carry

    lax.fori_loop(1, n - 1, one, 0)
    for part, (which, way, start, _, size) in enumerate(pieces):
        slot = slot_of(n - 2, part)
        copy_of(n - 2, part, slot).wait_recv()
        columns = pl.ds(start, size)
        o_refs[which][:, columns] = slot[...].astype(jnp.float32) + g_refs[which][
            me, :, columns
        ].astype(jnp.float32)

    def drain(step, carry):
        for part in range(len(pieces)):
            copy_of(step, part, slot_of(step, part)).wait_send()
        return carry

    lax.fori_loop(0, n - 1, drain, 0)


def ring_sum(gs, plan, axis, ident):
    n, rows, _ = gs[0].shape
    pieces, at = [], 0
    for which, way, start, size in plan:
        pieces.append((which, way, start, at, size))
        at += size
    return pl.pallas_call(
        functools.partial(ring_sum_kernel, n, axis, tuple(pieces), len(gs)),
        out_shape=tuple(jax.ShapeDtypeStruct(g.shape[1:], jnp.float32) for g in gs),
        in_specs=[pl.BlockSpec(memory_space=pltpu.VMEM)] * len(gs),
        out_specs=tuple(pl.BlockSpec(memory_space=pltpu.VMEM) for _ in gs),
        scratch_shapes=[
            pltpu.VMEM((n - 1, rows, at), gs[0].dtype),
            pltpu.SemaphoreType.DMA((n - 1, len(pieces))),
            pltpu.SemaphoreType.DMA((n - 1, len(pieces))),
        ],
        compiler_params=pltpu.CompilerParams(collective_id=ident, has_side_effects=True),
    )(*gs)


def scatter_sum_kernel(axis, x_ref, o_ref, near, far, total, send_sem, recv_sem):
    me, beside, across = quad(axis)
    greet((axis, beside), (axis, across))
    half = o_ref.shape[0] // 2
    parts = [pl.ds(0, half), pl.ds(half, half)]

    def pair(i, k, chunk):
        return remote(
            x_ref.at[chunk, parts[i]],
            near.at[k, parts[i]],
            send_sem.at[i, k],
            recv_sem.at[i, k],
            axis,
            beside,
        )

    copies = [pair(i, 0, (beside + 2) % 4) for i in range(2)]
    copies += [pair(i, 1, beside) for i in range(2)]
    for copy in copies:
        copy.start()
    crossing = []
    for i, rows in enumerate(parts):
        copies[i].wait_recv()
        total[rows] = (
            x_ref[across, rows].astype(jnp.float32) + near[0, rows].astype(jnp.float32)
        ).astype(total.dtype)
        copy = remote(
            total.at[rows], far.at[rows], send_sem.at[i, 2], recv_sem.at[i, 2], axis, across
        )
        copy.start()
        crossing.append(copy)
    for i, rows in enumerate(parts):
        copies[2 + i].wait_recv()
        crossing[i].wait_recv()
        o_ref[rows] = (
            x_ref[me, rows].astype(jnp.float32)
            + near[1, rows].astype(jnp.float32)
            + far[rows].astype(jnp.float32)
        )
    for copy in copies + crossing:
        copy.wait_send()


def scatter_sum(x, axis, ident):
    rows, columns = x.shape[0] // 4, x.shape[1]
    return pl.pallas_call(
        functools.partial(scatter_sum_kernel, axis),
        out_shape=jax.ShapeDtypeStruct((rows, columns), jnp.float32),
        in_specs=[pl.BlockSpec(memory_space=pltpu.VMEM)],
        out_specs=pl.BlockSpec(memory_space=pltpu.VMEM),
        scratch_shapes=[
            pltpu.VMEM((2, rows, columns), x.dtype),
            pltpu.VMEM((rows, columns), x.dtype),
            pltpu.VMEM((rows, columns), x.dtype),
            pltpu.SemaphoreType.DMA((2, 3)),
            pltpu.SemaphoreType.DMA((2, 3)),
        ],
        compiler_params=pltpu.CompilerParams(collective_id=ident, has_side_effects=True),
    )(x.reshape(4, rows, columns))


def chain(decay, state, first, last, backward, ident):
    n = lax.axis_size(SHARD)
    me = lax.axis_index(SHARD)
    lines = jnp.zeros((16, DV), jnp.float32)
    lines = lines.at[0, :DK].set(decay).at[1, 0].set(first).at[1, 1].set(last)
    block = jnp.concatenate([state, lines], axis=0).astype(jnp.bfloat16)
    every = ring_gather(block, SHARD, ident)
    states = every[:, :DK].astype(jnp.float32)
    decays = every[:, DK, :DK].astype(jnp.float32)
    firsts = every[:, DK + 1, 0].astype(jnp.float32)
    lasts = every[:, DK + 1, 1].astype(jnp.float32)
    place = jnp.arange(n)
    j, i = place[:, None], place[None, :]
    if backward:
        passing = decays
        between = jnp.logical_and(i > me, i < j)
        counted = place > me
    else:
        before = jnp.concatenate([jnp.zeros((1,), jnp.float32), lasts[:-1]])
        passing = decays * (firsts == before).astype(jnp.float32)[:, None]
        between = jnp.logical_and(i > j, i < me)
        counted = place < me
    weight = jnp.prod(jnp.where(between[:, :, None], passing[None], 1.0), axis=1)
    weight = jnp.where(counted[:, None], weight, 0.0)
    incoming = jnp.sum(weight[:, :, None] * states, axis=0)
    prior = jnp.sum(jnp.where(place == me - 1, lasts, 0.0))
    return incoming[None], prior


def rms_scale(values):
    return lax.rsqrt(jnp.mean(values * values, axis=-1, keepdims=True) + EPS)


def running(values):
    place = jnp.arange(values.shape[0])
    below = (place[:, None] >= place[None, :]).astype(jnp.float32)
    return jnp.einsum("ts,shk->thk", below, values, precision=HIGH_PRECISION)


def group_pass(query, key, value_rows, logdec, segf, state, carry_seg):
    total = query.shape[0]
    heads = query.shape[1]
    count = total // GROUP
    scale = DK ** (-0.5)
    order = jnp.arange(GROUP)
    causal = order[:, None] >= order[None, :]

    def blocks(array):
        return array.reshape((count, GROUP) + array.shape[1:])

    def advance(carry, pieces):
        memory_state, prior = carry
        query_c, key_c, value_segment, decay_c, seg_c = pieces
        cumul = running(decay_c)
        query_decayed = query_c * jnp.exp(cumul) * scale
        key_inc = key_c * jnp.exp(-cumul)
        scores = jnp.einsum("thk,shk->hts", query_decayed, key_inc, precision=HIGH_PRECISION)
        joined = jnp.logical_and(causal, seg_c[:, None] == seg_c[None, :])
        scores = jnp.where(joined[None], scores, 0.0)
        inherit = (seg_c == prior).astype(jnp.float32)
        inside = jnp.einsum("hts,shv->thv", scores, value_segment, precision=HIGH_PRECISION)
        carried_state = jnp.einsum(
            "zsb,sbi->zsi", query_decayed, memory_state, precision=HIGH_PRECISION
        )
        result = inside + inherit[:, None, None] * carried_state
        final_result = cumul[-1]
        keep = (seg_c == seg_c[-1]).astype(jnp.float32)
        key_final_rows = key_c * jnp.exp(final_result[None] - cumul) * keep[:, None, None]
        linked_states = (seg_c[-1] == prior).astype(jnp.float32)
        memory_state = linked_states * jnp.exp(final_result)[
            :, :, None
        ] * memory_state + jnp.einsum(
            "zie,zir->ier", key_final_rows, value_segment, precision=HIGH_PRECISION
        )
        return ((memory_state, seg_c[-1]), result)

    (memory_state, last_seg), outs = lax.scan(
        advance,
        (state, carry_seg),
        (blocks(query), blocks(key), blocks(value_rows), blocks(logdec), blocks(segf)),
        unroll=True,
    )
    return (outs.reshape(total, heads, outs.shape[-1]), memory_state)


def split_up(
    resid_in,
    cotangent,
    segment,
    attn_gain,
    w_query,
    w_key,
    w_value,
    w_outgate,
    w_low,
    w_rank,
    rank_bias,
    head_gain,
    w_out,
    mlp_gain,
    w_gate,
    w_up,
    w_down,
):

    n = lax.axis_size(SHARD)
    wide = w_gate.shape[1]
    rows = w_query.shape[0]

    def tall(a):
        a = a.reshape(a.shape[0], -1)
        return jnp.pad(a, ((0, rows - a.shape[0]), (0, 0)))

    packed = jnp.concatenate(
        [
            w_query,
            w_key,
            w_value,
            w_outgate,
            w_out.T,
            w_gate,
            w_up,
            w_down.T,
            w_low,
            tall(attn_gain),
            tall(mlp_gain),
            tall(head_gain),
            tall(w_rank[:, 0, :].T),
            tall(rank_bias[0]),
        ],
        axis=1,
    )
    used = packed.shape[1]
    packed = jnp.pad(packed, ((0, 0), (0, -used % LANE)))
    inv_attn = rms_scale(resid_in)
    unit_rows = (resid_in * inv_attn).astype(jnp.bfloat16)
    cot_rows = cotangent.astype(jnp.bfloat16)
    every, both = enter(packed, jnp.concatenate([unit_rows, cot_rows], axis=1), 1)
    spread = every.reshape(n * rows, packed.shape[1])
    edge_out = 2 * DK + 2 * DV
    edge_gate = edge_out + DV
    edge_down = edge_gate + 2 * wide
    edge_low = edge_down + wide
    project_w = spread[:, :edge_out]
    out_wt = spread[:, edge_out:edge_gate]
    gu_w = spread[:, edge_gate:edge_down]
    down_wt = spread[:, edge_down:edge_low]
    tail = every[:, :, edge_low:]
    low_w = tail[:, :, :GATE_RANK].reshape(D, GATE_RANK)
    gain_attn = tail[:, :, GATE_RANK].reshape(D).astype(jnp.float32)
    gain_mlp = tail[:, :, GATE_RANK + 1].reshape(D).astype(jnp.float32)
    gain_head = tail[:, : DV // n, GATE_RANK + 2].reshape(DV).astype(jnp.float32)
    rank_w = tail[:, : DK // n, GATE_RANK + 3 : 2 * GATE_RANK + 3].reshape(DK, GATE_RANK).T
    bias_w = tail[:, : DK // n, 2 * GATE_RANK + 3].reshape(DK)
    length = segment.shape[0]
    local_heads = 1
    scale = DK ** (-0.5)
    normed_in = (
        (both[:, :, :D].astype(jnp.float32) * gain_attn).astype(jnp.bfloat16).reshape(length, D)
    )
    cot_bf = both[:, :, D:].reshape(length, D)
    projected = jnp.dot(normed_in, project_w, preferred_element_type=jnp.float32)
    query = projected[:, :DK].reshape(length, local_heads, DK)
    key = projected[:, DK : 2 * DK].reshape(length, local_heads, DK)
    value_rows = projected[:, 2 * DK : 2 * DK + DV].reshape(length, local_heads, DV)
    outgate = projected[:, 2 * DK + DV :].reshape(length, local_heads, DV)
    low = jnp.dot(normed_in, low_w, preferred_element_type=jnp.float32)
    rank_mat = rank_w.astype(jnp.float32).reshape(GATE_RANK, local_heads * DK)
    logit = jnp.dot(low, rank_mat, precision=HIGH_PRECISION) + bias_w.astype(jnp.float32).reshape(
        local_heads * DK
    )
    logdec = (jax.nn.log_sigmoid(logit) / 16.0).reshape(length, local_heads, DK)
    segf = segment.astype(jnp.float32) + 1.0
    first_seg = segf[:1]
    last_seg = segf[-1:]
    cumul = running(logdec)
    keep = (segf == last_seg[0]).astype(jnp.float32)
    key_final_rows = key * jnp.exp(cumul[-1][None] - cumul) * keep[:, None, None]
    summary_state = jnp.einsum("zie,zir->ier", key_final_rows, value_rows, precision=HIGH_PRECISION)
    through = jnp.exp(cumul[-1]) * (first_seg[0] == last_seg[0]).astype(jnp.float32)
    state_in, prior = chain(through[0], summary_state[0], first_seg[0], last_seg[0], False, 3)

    def mixer(query_in, key_in, value_in, decay_in):
        return group_pass(query_in, key_in, value_in, decay_in, segf, state_in, prior)

    (mixed, state_out), mixer_back = jax.vjp(mixer, query, key, value_rows, logdec)
    inv_head = rms_scale(mixed)
    headnormed = mixed * inv_head * gain_head
    sigma_out = jax.nn.sigmoid(outgate)
    swish_out = outgate * sigma_out
    gated = (headnormed * swish_out).reshape(length, local_heads * DV).astype(jnp.bfloat16)
    resid_mid = resid_in + scatter_sum(
        jnp.dot(gated, out_wt.T, preferred_element_type=jnp.float32).astype(jnp.bfloat16),
        HEAD,
        4,
    )
    inv_mlp = rms_scale(resid_mid)
    mid_rows = (resid_mid * inv_mlp * gain_mlp).astype(jnp.bfloat16)
    normed_mid = gather(mid_rows, HEAD, 5).reshape(length, D)
    gate_up = jnp.dot(normed_mid, gu_w, preferred_element_type=jnp.float32)
    gate_pre = gate_up[:, :wide]
    up_pre = gate_up[:, wide:]
    sigma_gate = jax.nn.sigmoid(gate_pre)
    active = gate_pre * sigma_gate
    hidden = (active * up_pre).astype(jnp.bfloat16)
    d_hidden = jnp.dot(cot_bf, down_wt, preferred_element_type=jnp.float32)
    d_gatepre = (d_hidden * up_pre * sigma_gate * (1.0 + gate_pre * (1.0 - sigma_gate))).astype(
        jnp.bfloat16
    )
    d_uppre = (d_hidden * active).astype(jnp.bfloat16)
    d_gu = jnp.concatenate([d_gatepre, d_uppre], axis=1)
    grad_down = jnp.dot(cot_bf.T, hidden, preferred_element_type=jnp.float32)
    grad_gu = jnp.dot(normed_mid.T, d_gu, preferred_element_type=jnp.float32)
    shares = jnp.concatenate(
        [
            jnp.dot(hidden, down_wt.T, preferred_element_type=jnp.float32).astype(jnp.bfloat16),
            jnp.dot(d_gu, gu_w.T, preferred_element_type=jnp.float32).astype(jnp.bfloat16),
        ],
        axis=1,
    )
    summed = scatter_sum(shares, HEAD, 6)
    resid_out = resid_mid + summed[:, :D]
    d_normmid = summed[:, D:]
    part_mlp_gain = jnp.sum(d_normmid * resid_mid * inv_mlp, axis=0)
    scaled_mid = gain_mlp * d_normmid
    d_mid = (
        cotangent
        + inv_mlp * scaled_mid
        - resid_mid * inv_mlp**3 * jnp.mean(scaled_mid * resid_mid, axis=-1, keepdims=True)
    )
    dmid_rows = d_mid.astype(jnp.bfloat16)
    dmid_bf = gather(dmid_rows, HEAD, 7).reshape(length, D)
    d_gated = jnp.dot(dmid_bf, out_wt, preferred_element_type=jnp.float32).reshape(
        length, local_heads, DV
    )
    grad_out = jnp.dot(dmid_bf.T, gated, preferred_element_type=jnp.float32)
    d_head = d_gated * swish_out
    d_outgate = (
        (d_gated * headnormed * sigma_out * (1.0 + outgate * (1.0 - sigma_out)))
        .reshape(length, local_heads * DV)
        .astype(jnp.bfloat16)
    )
    part_head_gain = jnp.sum(d_head * mixed * inv_head, axis=(0, 1))
    scaled_head = gain_head * d_head
    mixed_gradient = inv_head * scaled_head - mixed * inv_head**3 * jnp.mean(
        scaled_head * mixed, axis=-1, keepdims=True
    )
    inherit = (segf == prior).astype(jnp.float32)
    weighted_query = query * jnp.exp(cumul) * inherit[:, None, None] * scale
    local_gradient = jnp.einsum(
        "zie,zir->ier", weighted_query, mixed_gradient, precision=HIGH_PRECISION
    )
    through_all = jnp.exp(cumul[-1]) * (last_seg[0] == prior).astype(jnp.float32)
    nothing = jnp.zeros((), jnp.float32)
    outgoing, _ = chain(through_all[0], local_gradient[0], nothing, nothing, True, 8)
    d_query, d_key, d_value, d_logdec = mixer_back((mixed_gradient, outgoing))
    query_bf = d_query.reshape(length, local_heads * DK).astype(jnp.bfloat16)
    key_bf = d_key.reshape(length, local_heads * DK).astype(jnp.bfloat16)
    value_bf = d_value.reshape(length, local_heads * DV).astype(jnp.bfloat16)
    d_logit = d_logdec.reshape(length, local_heads * DK) * jax.nn.sigmoid(-logit) / 16.0
    grad_bias = jnp.sum(d_logit, axis=0).reshape(local_heads, DK)
    grad_rank = jnp.dot(low.T, d_logit, precision=HIGH_PRECISION).reshape(
        GATE_RANK, local_heads, DK
    )
    d_low = (
        jnp.einsum(
            "thk,rhk->thr",
            d_logit.reshape(length, local_heads, DK),
            rank_w.astype(jnp.float32).reshape(GATE_RANK, local_heads, DK),
            precision=HIGH_PRECISION,
        )
        .astype(jnp.bfloat16)
        .reshape(length, local_heads * GATE_RANK)
    )
    part_low = (
        jnp.dot(normed_in.T, d_low, preferred_element_type=jnp.float32)
        .reshape(D, local_heads, GATE_RANK)
        .sum(axis=1)
    )
    d_project = jnp.concatenate([query_bf, key_bf, value_bf, d_outgate], axis=1)
    grad_project = jnp.dot(normed_in.T, d_project, preferred_element_type=jnp.float32)
    low_rows = low_w.T
    total_term = jnp.dot(d_project, project_w.T, preferred_element_type=jnp.float32)
    d_normin = scatter_sum(
        (total_term + jnp.dot(d_low, low_rows, preferred_element_type=jnp.float32)).astype(
            jnp.bfloat16
        ),
        HEAD,
        9,
    )
    part_attn_gain = jnp.sum(d_normin * resid_in * inv_attn, axis=0)
    scaled_in = gain_attn * d_normin
    grad_in = (
        d_mid
        + inv_attn * scaled_in
        - resid_in * inv_attn**3 * jnp.mean(scaled_in * resid_in, axis=-1, keepdims=True)
    )

    def owners(a):
        a = a.reshape(n, a.shape[0] // n, -1)
        return jnp.pad(a, ((0, 0), (0, rows - a.shape[1]), (0, 0))).reshape(D, -1)

    lean = jnp.concatenate(
        [
            part_low,
            part_attn_gain[:, None],
            part_mlp_gain[:, None],
            owners(part_head_gain),
            owners(grad_rank[:, 0, :].T),
            owners(grad_bias[0]),
        ],
        axis=1,
    )
    lean = jnp.pad(lean, ((0, 0), (0, packed.shape[1] - used)))
    grads = [
        g.astype(jnp.bfloat16).reshape(n, rows, -1)
        for g in (
            grad_project,
            grad_out,
            grad_gu,
            jnp.concatenate([grad_down, lean], axis=1),
        )
    ]
    middle = (wide // LANE + 1) * LANE
    plan = (
        (2, 0, 0, middle),
        (3, 1, 0, grads[3].shape[2]),
        (0, 0, 0, edge_out),
        (2, 1, middle, 2 * wide - middle),
        (1, 1, 0, DV),
    )
    own_project, own_out, own_gu, own_rest = ring_sum(grads, plan, SHARD, 10)
    heads = lax.axis_size(HEAD)
    shared = own_rest[:, wide : wide + GATE_RANK + 3]
    gain_rows = DV // n
    final_rank = own_rest[: DK // n, wide + GATE_RANK + 3 : wide + 2 * GATE_RANK + 3]
    final_bias = own_rest[: DK // n, wide + 2 * GATE_RANK + 3]
    shares = jnp.concatenate(
        [
            shared[:, : GATE_RANK + 2].reshape(heads, rows // heads, GATE_RANK + 2),
            jnp.pad(
                shared[:gain_rows, GATE_RANK + 2].reshape(heads, gain_rows // heads, 1),
                ((0, 0), (0, (rows - gain_rows) // heads), (0, 0)),
            ),
        ],
        axis=2,
    )
    deep = max(rows // heads, 32)
    shares = jnp.pad(
        shares, ((0, 0), (0, deep - rows // heads), (0, LANE - GATE_RANK - 3))
    ).reshape(heads * deep, LANE)
    final = scatter_sum(shares.astype(jnp.bfloat16), HEAD, 11)[: rows // heads]
    return (
        resid_out,
        grad_in,
        final[:, GATE_RANK],
        own_project[:, :DK],
        own_project[:, DK : 2 * DK],
        own_project[:, 2 * DK : 2 * DK + DV],
        own_project[:, 2 * DK + DV :],
        final[:, :GATE_RANK],
        final_rank.T.reshape(GATE_RANK, 1, DK // n),
        final_bias.reshape(1, DK // n),
        final[: gain_rows // heads, GATE_RANK + 2],
        own_out.T,
        final[:, GATE_RANK + 1],
        own_gu[:, :wide],
        own_gu[:, wide:],
        own_rest[:, :wide].T,
    )


SEQ = 1024
NN = ((1,), (0,))
NT = ((1,), (1,))
TN = ((0,), (0,))
SMALL = 48
F32 = jnp.float32
BF16 = jnp.bfloat16


def mm(a, b, dims, precision=None):
    return lax.dot_general(
        a, b, (dims, ((), ())), precision=precision, preferred_element_type=F32
    )


def exact(a, b, dims):
    return mm(a, b, dims, HIGH_PRECISION)


def quad_gather(buf, send_sem, recv_sem):
    me, beside, across = quad(HEAD)
    half = buf.shape[1] // 2
    first, onward = [], []
    for i in range(2):
        rows = pl.ds(i * half, half)
        own, got = buf.at[me, rows], buf.at[across, rows]
        far = remote(own, own, send_sem.at[i, 0], recv_sem.at[i, 0], HEAD, across)
        near = remote(own, own, send_sem.at[i, 1], recv_sem.at[i, 1], HEAD, beside)
        more = remote(got, got, send_sem.at[i, 2], recv_sem.at[i, 2], HEAD, beside)
        first.append((far, near))
        onward.append(more)

    def start():
        for far, near in first:
            far.start()
            near.start()

    def relay():
        for (far, _), more in zip(first, onward):
            far.wait_recv()
            more.start()

    def finish():
        for (_, near), more in zip(first, onward):
            near.wait_recv()
            more.wait_recv()

    def drain():
        for (far, near), more in zip(first, onward):
            far.wait_send()
            near.wait_send()
            more.wait_send()

    return start, relay, finish, drain


def quad_sum(part, near, far, total, send_sem, recv_sem):
    me, beside, across = quad(HEAD)
    half = part.shape[1] // 2
    parts = [pl.ds(i * half, half) for i in range(2)]

    def pair(i, k, chunk):
        return remote(
            part.at[chunk, parts[i]],
            near.at[k, parts[i]],
            send_sem.at[i, k],
            recv_sem.at[i, k],
            HEAD,
            beside,
        )

    copies = [pair(i, 0, (beside + 2) % 4) for i in range(2)]
    copies += [pair(i, 1, beside) for i in range(2)]
    crossing = [
        remote(total.at[rows], far.at[rows], send_sem.at[i, 2], recv_sem.at[i, 2], HEAD, across)
        for i, rows in enumerate(parts)
    ]

    def start():
        for copy in copies:
            copy.start()

    def cross():
        for i, rows in enumerate(parts):
            copies[i].wait_recv()
            total[rows] = (part[across, rows].astype(F32) + near[0, rows].astype(F32)).astype(BF16)
            crossing[i].start()

    def finish():
        for i in range(2):
            copies[2 + i].wait_recv()
            crossing[i].wait_recv()
        return part[me].astype(F32) + near[1].astype(F32) + far[...].astype(F32)

    def drain():
        for copy in copies + crossing:
            copy.wait_send()

    return start, cross, finish, drain


class Refs(dict):
    __getattr__ = dict.__getitem__


def block_kernel(n, reach, names, *refs):
    r = Refs(zip(names, refs))
    s = lax.axis_index(SHARD)
    me = lax.axis_index(HEAD)
    _, beside, across = quad(HEAD)
    opposite = (beside + 2) % 4
    pos = ring_place(s, n)
    right, left = ring_sides(n, SHARD)
    steps = n // 2
    wide = r.w_down.shape[0]
    part = wide // 2
    length = r.segment.shape[1]
    groups = length // GROUP
    wp, wd = r.wp, r.wd
    at_out = SMALL
    at_gate = at_out + DV
    at_up = at_gate + wide
    at_down = at_up + wide
    depth = wp.shape[0] // n

    def lanes(b):
        return pl.ds(pl.multiple_of(b * LANE, LANE), LANE)

    def rows_of(b, start, size):
        return pl.ds(pl.multiple_of(b * depth + start, 16), size)

    ag_pieces = []

    def add_rows(start, size, last):
        ag_pieces.append((None, lambda b: wp.at[rows_of(b, start, size)], last))

    def add_lanes(ref, start, size, at, last):
        ag_pieces.append(
            (ref.at[pl.ds(start, size)], lambda b: wd.at[pl.ds(at + start, size), lanes(b)], last)
        )

    add_rows(0, depth // 2, 0)
    add_rows(depth // 2, depth // 2, 1)
    add_lanes(r.small, 0, SMALL, 0, 0)
    add_lanes(r.w_out, 0, DV // 2, at_out, 0)
    add_lanes(r.w_out, DV // 2, DV // 2, at_out, 1)
    add_lanes(r.w_gate, 0, part, at_gate, 0)
    add_lanes(r.w_gate, part, part, at_gate, 1)
    add_lanes(r.w_up, 0, part, at_up, 0)
    add_lanes(r.w_up, part, part, at_up, 1)
    add_lanes(r.w_down, 0, part, at_down, 0)
    add_lanes(r.w_down, part, part, at_down, 1)

    def ag_copy(p, step, way):
        own, place, _ = ag_pieces[p]
        shift = n - step if way == 0 else step
        b = ring_index((pos + shift) % n, n)
        source = own if step == 0 and own is not None else place(b)
        return remote(
            source,
            place(b),
            r.ag_send.at[p, way, step],
            r.ag_recv.at[p, way, step],
            SHARD,
            right if way == 0 else left,
        )

    def ag_has(p, step, way):
        return step < steps - 1 or ag_pieces[p][2] == way

    def ag(ps, step):
        for p in ps:
            for way in range(2):
                if ag_has(p, step, way):
                    if step > 0:
                        ag_copy(p, step - 1, way).wait_recv()
                    ag_copy(p, step, way).start()

    def ag_finish(ps):
        for p in ps:
            for way in range(2):
                if ag_has(p, steps - 1, way):
                    ag_copy(p, steps - 1, way).wait_recv()
                else:
                    ag_copy(p, steps - 2, way).wait_recv()

    def ag_drain():
        for p in range(len(ag_pieces)):
            for step in range(steps):
                for way in range(2):
                    if ag_has(p, step, way):
                        ag_copy(p, step, way).wait_send()

    gm, go, gp = r.gm, r.go, r.gp
    rs_pieces = []
    for start, out in ((0, (r.v_down, r.g_down)), (wide, (r.v_gate, r.g_gate)), (2 * wide, (r.v_up, r.g_up))):
        for way in range(2):
            rs_pieces.append((gm, r.held_m, start + way * part, part, way, (out, way * part)))
    for way in range(2):
        rs_pieces.append((go, r.held_o, way * (DV // 2), DV // 2, way, ((r.v_out, r.g_out), way * (DV // 2))))
    for i in range(4):
        q = depth // 4
        rs_pieces.append((gp, r.held_p, i * q, q, i % 2, ((r.v_proj, None), i * q)))
    DOWN, GATE, UP, OUT, PROJ = (0, 1), (2, 3), (4, 5), (6, 7), (8, 9, 10, 11)

    def rs_own(p, step):
        g, _, start, size, way, _ = rs_pieces[p]
        shift = 2 * n - 1 - step if way == 0 else 1 + step
        return g.at[ring_index((pos + shift) % n, n), pl.ds(start, size)]

    def rs_slot(p, step):
        _, held, start, size, _, _ = rs_pieces[p]
        return held.at[step, pl.ds(start, size)]

    def rs_copy(p, step):
        source = rs_own(p, 0) if step == 0 else rs_slot(p, step - 1)
        return remote(
            source,
            rs_slot(p, step),
            r.rs_send.at[p, step],
            r.rs_recv.at[p, step],
            SHARD,
            right if rs_pieces[p][4] == 0 else left,
        )

    def rs(ps, step):
        for p in ps:
            if step > 0:
                rs_copy(p, step - 1).wait_recv()
                slot = rs_slot(p, step - 1)
                slot[...] = (slot[...].astype(F32) + rs_own(p, step)[...].astype(F32)).astype(BF16)
            rs_copy(p, step).start()

    written = []

    def emit(source, target):
        copy = pltpu.make_async_copy(source, target, r.out_sem.at[len(written)])
        copy.start()
        written.append(copy)

    def rs_finish(ps):
        for p in ps:
            rs_copy(p, n - 2).wait_recv()
            total = rs_slot(p, n - 2)[...].astype(F32) + rs_own(p, n - 1)[...].astype(F32)
            (held, out), start = rs_pieces[p][5]
            rows = pl.ds(start, rs_pieces[p][3])
            held[rows, :] = total
            if out is not None:
                emit(held.at[rows], out.at[rows])
            else:
                at = 0
                for out, width in ((r.g_query, DK), (r.g_key, DK), (r.g_value, DV), (r.g_outgate, DV)):
                    emit(held.at[rows, pl.ds(at, width)], out.at[rows])
                    at += width

    def rs_drain():
        for p in range(len(rs_pieces)):
            for step in range(n - 1):
                rs_copy(p, step).wait_send()

    def chain_copy(which, d):
        send, got = r.chain_send, r.chain_recv
        peer = s + d if which == 0 else s - d
        return remote(
            send.at[which],
            got.at[which, d - 1],
            r.chain_ssem.at[which, d - 1],
            r.chain_rsem.at[which, d - 1],
            SHARD,
            peer,
        )

    def has_peer(which, d):
        return s + d < n if which == 0 else s - d >= 0

    def chain_start(which):
        for d in range(1, reach + 1):
            pl.when(has_peer(which, d))(lambda d=d: chain_copy(which, d).start())

    def chain_wait(which):
        for d in range(1, reach + 1):
            pl.when(has_peer(1 - which, d))(lambda d=d: chain_copy(which, d).wait_recv())

    def chain_drain(which):
        for d in range(1, reach + 1):
            pl.when(has_peer(which, d))(lambda d=d: chain_copy(which, d).wait_send())

    def chain_sum(which):
        got = r.chain_recv
        total = got[which, 0, pl.ds(0, DV)].astype(F32)
        weight = None
        for d in range(2, reach + 1):
            lines = got[which, d - 2, pl.ds(DV, 16)].astype(F32)
            link = lines[0:1]
            if which == 0:
                before = got[which, d - 1, pl.ds(DV, 16)].astype(F32)[2:3]
                link = link * (lines[1:2] == before).astype(F32)
            weight = link if weight is None else weight * link
            total = total + weight * got[which, d - 1, pl.ds(0, DV)].astype(F32)
        return total

    def lines_of(*rows):
        rows = list(rows) + [jnp.zeros((16 - len(rows), DK), F32)]
        return jnp.concatenate(rows, axis=0).astype(BF16)

    gather_x = quad_gather(r.x4, r.qg_send.at[0], r.qg_recv.at[0])
    gather_c = quad_gather(r.cot4, r.qg_send.at[1], r.qg_recv.at[1])
    gather_m = quad_gather(r.mid4, r.qg_send.at[2], r.qg_recv.at[2])
    gather_d = quad_gather(r.dmid4, r.qg_send.at[3], r.qg_recv.at[3])

    def summing(i, tag):
        return quad_sum(
            r["part_" + tag],
            r["near_" + tag],
            r["far_" + tag],
            r["total_" + tag],
            r.qs_send.at[i],
            r.qs_recv.at[i],
        )

    sum_o, sum_m, sum_i = summing(0, "o"), summing(1, "m"), summing(2, "i")

    own_lanes = lanes(s)
    own_rows = rows_of(s, 0, depth)
    moves = [
        (r.resid_in, r.x_in),
        (r.w_low, r.s_low),
        (r.w_rank, r.s_rank),
        (r.attn_gain, r.s_attn),
        (r.mlp_gain, r.s_mlp),
        (r.head_gain, r.s_head),
        (r.rank_bias, r.s_bias),
        (r.w_query, wp.at[own_rows, pl.ds(0, DK)]),
        (r.w_key, wp.at[own_rows, pl.ds(DK, DK)]),
        (r.w_value, wp.at[own_rows, pl.ds(2 * DK, DV)]),
        (r.w_outgate, wp.at[own_rows, pl.ds(2 * DK + DV, DV)]),
        (r.cotangent, r.cot_in),
        (r.segment, r.seg_in),
        (r.w_out, wd.at[pl.ds(at_out, DV), own_lanes]),
        (r.w_gate, wd.at[pl.ds(at_gate, wide), own_lanes]),
        (r.w_up, wd.at[pl.ds(at_up, wide), own_lanes]),
        (r.w_down, wd.at[pl.ds(at_down, wide), own_lanes]),
    ]
    own = [pltpu.make_async_copy(a, b, r.own_sem.at[i]) for i, (a, b) in enumerate(moves)]
    for copy in own:
        copy.start()
    barrier = pltpu.get_barrier_semaphore()
    r.chain_recv[...] = jnp.zeros_like(r.chain_recv)
    for d in range(1, n):
        pl.semaphore_signal(barrier, inc=1, device_id={SHARD: (s + d) % n}, device_id_type=MESH)
    for peer in (beside, across, opposite):
        pl.semaphore_signal(barrier, inc=1, device_id={HEAD: peer}, device_id_type=MESH)
    own[0].wait()
    inv_attn = rms_scale(r.x_in[...])
    r.x4[me] = r.x_in[...] * inv_attn
    for copy in own[1:11]:
        copy.wait()
    part_k, part_v = DK // n, DV // n
    pad = r.pad
    pad[...] = jnp.zeros_like(pad)
    pad[0:GATE_RANK, 0:part_k] = r.s_rank[...].astype(F32)
    pad[16:17, 0:part_k] = r.s_bias[...].astype(F32)
    pad[24:25, 0:part_v] = r.s_head[...].astype(F32)
    by_k = pltpu.roll(pad[0:24], s * part_k, 1)
    by_v = pltpu.roll(pad[24:32], (s * part_v) % LANE, 1)[0:1]
    lower = (lax.broadcasted_iota(jnp.int32, (1, LANE), 1) * 0 + s) < n // 2
    r.small[0:16] = r.s_low[...]
    r.small[16:32] = by_k[0:16].astype(BF16)
    r.small[32:48] = jnp.concatenate(
        [
            r.s_attn[...].astype(F32),
            r.s_mlp[...].astype(F32),
            jnp.where(lower, by_v, 0.0),
            jnp.where(lower, 0.0, by_v),
            by_k[16:17],
            jnp.zeros((11, LANE), F32),
        ],
        axis=0,
    ).astype(BF16)
    wd[pl.ds(0, SMALL), own_lanes] = r.small[...]
    pl.semaphore_wait(barrier, n + 2)

    P0, WO, GU, DN = (0, 1, 2), (3, 4), (5, 6, 7, 8), (9, 10)
    ag(P0, 0)
    gather_x[0]()
    own[11].wait()
    r.cot4[me] = r.cot_in[...].astype(BF16)
    ag(WO, 0)
    gather_x[1]()
    ag(P0, 1)
    gather_c[0]()
    ag(P0, 2)
    ag(WO, 1)
    ag(P0, 3)
    ag(GU, 0)
    gather_x[2]()
    gather_c[1]()
    for copy in own[12:]:
        copy.wait()
    ag_finish(P0)

    fine = wd[pl.ds(32, 16), :].astype(F32)
    gain_attn, gain_mlp = fine[0:1], fine[1:2]

    def folded(block):
        total = block[:, 0:LANE]
        for b in range(1, n):
            total = total + block[:, b * LANE : (b + 1) * LANE]
        return total

    tiny = folded(fine)
    gain_head = jnp.concatenate([tiny[2:3], tiny[3:4]], axis=1)
    bias = tiny[4:5]
    rank = folded(wd[pl.ds(16, 16), :].astype(F32))
    normed = (r.x4[...].reshape(length, D) * gain_attn).astype(BF16)
    r.normed[...] = normed
    proj = r.proj
    low = mm(normed, wd[pl.ds(0, 16), :], NT)
    r.low[...] = low
    logit = exact(low, rank, NN) + bias
    r.logit[...] = logit
    proj[:, 0 : 2 * DK + DV] = mm(normed, wp[:, 0 : 2 * DK + DV], NN)
    logdec = (jnp.minimum(logit, 0.0) - jnp.log1p(jnp.exp(-jnp.abs(logit)))) / 16.0
    ti = lax.broadcasted_iota(jnp.int32, (length, length), 0)
    tj = lax.broadcasted_iota(jnp.int32, (length, length), 1)
    below = jnp.logical_and(ti // GROUP == tj // GROUP, ti >= tj)
    cumul = exact(below.astype(F32), logdec, NN)
    seg_row = r.seg_in[...].astype(F32) + 1.0
    seg_l = jnp.broadcast_to(seg_row, (DK, length)).T
    seg_wide = jnp.concatenate([seg_l] * (length // DK), axis=1)
    joined = jnp.logical_and(below, seg_wide == seg_row)
    scale = DK ** (-0.5)
    query, key = proj[:, 0:DK], proj[:, DK : 2 * DK]
    value = proj[:, 2 * DK : 2 * DK + DV]

    def group(a, c):
        return a[c * GROUP : (c + 1) * GROUP]

    ends = [cumul[(c + 1) * GROUP - 1 : (c + 1) * GROUP] for c in range(groups)]
    last_seg = [seg_l[(c + 1) * GROUP - 1 : (c + 1) * GROUP] for c in range(groups)]
    fade = jnp.concatenate(
        [
            jnp.exp(ends[c] - group(cumul, c)) * (group(seg_l, c) == last_seg[c]).astype(F32)
            for c in range(groups)
        ],
        axis=0,
    )
    key_final = key * fade
    dec = [jnp.exp(e) for e in ends]
    local = [None]
    for c in range(groups):
        update = exact(group(value, c), group(key_final, c), TN)
        if c > 0:
            linked = dec[c] * (last_seg[c] == last_seg[c - 1]).astype(F32)
            update = update + linked * local[c]
        local.append(update)
    whole_end = ends[0]
    for e in ends[1:]:
        whole_end = whole_end + e
    first_seg, final_seg = seg_l[0:1], last_seg[-1]
    through = jnp.exp(whole_end) * (first_seg == final_seg).astype(F32)
    r.chain_send[0, pl.ds(0, DV)] = local[groups].astype(BF16)
    r.chain_send[0, pl.ds(DV, 16)] = lines_of(through, first_seg, final_seg)
    chain_start(0)
    ag(WO, 2)
    ag(WO, 3)
    for c in range(1, groups):
        r.states[c] = local[c]
    r.fade[...] = fade
    r.seg_l[...] = seg_l
    grown = jnp.exp(cumul)
    r.grown[...] = grown
    query_dec = query * grown * scale
    shrunk = jnp.exp(-cumul)
    r.shrunk[...] = shrunk
    key_inc = key * shrunk
    r.query_dec[...] = query_dec
    r.key_inc[...] = key_inc
    scores = jnp.where(joined, exact(query_dec, key_inc, NT), 0.0)
    r.scores[...] = scores
    inside = exact(scores, value, NN)
    r.mixed[...] = inside
    outgate = mm(r.normed[...], wp[:, 2 * DK + DV : 2 * DK + 2 * DV], NN)
    proj[:, 2 * DK + DV : 2 * DK + 2 * DV] = outgate
    ag(GU, 1)
    chain_wait(0)
    state_in = chain_sum(0)
    prior = r.chain_recv[0, 0, pl.ds(DV, 16)].astype(F32)[2:3]
    before = [prior] + last_seg[:-1]
    r.prior[...] = jnp.broadcast_to(prior, (8, DK))
    decay = jnp.ones((1, DK), F32)
    for c in range(groups):
        if c == 0:
            state = state_in
        else:
            decay = decay * dec[c - 1]
            state = r.states[c] + decay * (last_seg[c - 1] == prior).astype(F32) * state_in
        r.states[c] = state
        inherit = (group(seg_l, c) == before[c]).astype(F32)
        r.mixed[pl.ds(c * GROUP, GROUP)] += exact(inherit * group(query_dec, c), state, NT)
    mixed = r.mixed[...]
    inv_head = rms_scale(mixed)
    gated = (mixed * inv_head * gain_head * (outgate * jax.nn.sigmoid(outgate))).astype(BF16)
    r.gated[...] = gated
    ag_finish(WO)
    r.part_o[...] = (
        mm(gated, wd[pl.ds(at_out, DV), :], NN).astype(BF16).reshape(r.part_o.shape)
    )
    sum_o[0]()
    ag(GU, 2)
    sum_o[1]()
    ag(DN, 0)
    gather_c[2]()
    resid_mid = r.x_in[...] + sum_o[2]()
    r.resid_mid[...] = resid_mid
    inv_mlp = rms_scale(resid_mid)
    r.mid4[me] = (resid_mid * inv_mlp * gain_mlp).astype(BF16)
    gather_m[0]()
    ag(GU, 3)
    gather_m[1]()
    ag(DN, 1)
    gather_m[2]()
    ag_finish(GU)

    normed_mid = r.mid4[...].reshape(length, D)
    cot_bf = r.cot4[...].reshape(length, D)
    r.gate_pre[...] = mm(wd[pl.ds(at_gate, wide), :], normed_mid, NT)
    ag(DN, 2)
    r.up_pre[...] = mm(wd[pl.ds(at_up, wide), :], normed_mid, NT)
    gate_pre = r.gate_pre[...]
    r.hidden[...] = (gate_pre * jax.nn.sigmoid(gate_pre) * r.up_pre[...]).astype(BF16)
    ag(DN, 3)

    def spread(g, at, size, value):
        for b in range(n):
            g[b, pl.ds(at, size)] = value[:, b * LANE : (b + 1) * LANE].astype(BF16)

    spread(gm, 0, wide, mm(r.hidden[...], cot_bf, NN))
    rs(DOWN, 0)
    ag_finish(DN)
    d_hidden = mm(wd[pl.ds(at_down, wide), :], cot_bf, NT)
    gate_pre, up_pre = r.gate_pre[...], r.up_pre[...]
    sigma = jax.nn.sigmoid(gate_pre)
    r.d_gate[...] = (d_hidden * up_pre * sigma * (1.0 + gate_pre * (1.0 - sigma))).astype(BF16)
    r.d_up[...] = (d_hidden * (gate_pre * sigma)).astype(BF16)
    spread(gm, wide, wide, mm(r.d_gate[...], normed_mid, NN))
    rs(GATE, 0)
    spread(gm, 2 * wide, wide, mm(r.d_up[...], normed_mid, NN))
    rs(UP, 0)
    r.part_m[:, :, 0:D] = (
        mm(r.hidden[...], wd[pl.ds(at_down, wide), :], TN).astype(BF16).reshape(4, length // 4, D)
    )
    r.part_m[:, :, D : 2 * D] = (
        (
            mm(r.d_gate[...], wd[pl.ds(at_gate, wide), :], TN)
            + mm(r.d_up[...], wd[pl.ds(at_up, wide), :], TN)
        )
        .astype(BF16)
        .reshape(4, length // 4, D)
    )
    sum_m[0]()
    rs(DOWN, 1)
    sum_m[1]()
    rs(GATE, 1)
    summed = sum_m[2]()
    resid_mid = r.resid_mid[...]
    r.v_resid[...] = resid_mid + summed[:, 0:D]
    emit(r.v_resid, r.resid_out)
    d_normmid = summed[:, D : 2 * D]
    inv_mlp = rms_scale(resid_mid)
    mlp_row = jnp.sum(d_normmid * resid_mid * inv_mlp, axis=0, keepdims=True)
    scaled = gain_mlp * d_normmid
    d_mid = (
        r.cot_in[...]
        + inv_mlp * scaled
        - resid_mid * inv_mlp**3 * jnp.mean(scaled * resid_mid, axis=-1, keepdims=True)
    )
    r.d_mid[...] = d_mid
    r.dmid4[me] = d_mid.astype(BF16)
    gather_d[0]()
    rs(UP, 1)
    rs(DOWN, 2)
    gather_d[1]()
    rs(GATE, 2)
    gather_d[2]()

    dmid_bf = r.dmid4[...].reshape(length, D)
    gated = r.gated[...]
    d_gated = mm(dmid_bf, wd[pl.ds(at_out, DV), :], NT)
    spread(go, 0, DV, mm(gated, dmid_bf, TN))
    rs(OUT, 0)
    outgate = proj[:, 2 * DK + DV : 2 * DK + 2 * DV]
    mixed = r.mixed[...]
    inv_head = rms_scale(mixed)
    sigma = jax.nn.sigmoid(outgate)
    d_head = d_gated * (outgate * sigma)
    r.d_proj[:, 2 * DK + DV : 2 * DK + 2 * DV] = (
        d_gated * (mixed * inv_head * gain_head) * sigma * (1.0 + outgate * (1.0 - sigma))
    ).astype(BF16)
    head_row = jnp.sum(d_head * mixed * inv_head, axis=0, keepdims=True)
    scaled = gain_head * d_head
    d_mixed = inv_head * scaled - mixed * inv_head**3 * jnp.mean(
        scaled * mixed, axis=-1, keepdims=True
    )
    query_dec, seg_l = r.query_dec[...], r.seg_l[...]
    prior = r.prior[0:1]
    last_seg = [seg_l[(c + 1) * GROUP - 1 : (c + 1) * GROUP] for c in range(groups)]
    before = [prior] + last_seg[:-1]
    grown = r.grown[...]
    dec = [
        grown[(c + 1) * GROUP - 1 : (c + 1) * GROUP] * (last_seg[c] == before[c]).astype(F32)
        for c in range(groups)
    ]
    pulls = []
    for c in range(groups):
        inherit = (group(seg_l, c) == before[c]).astype(F32)
        pulls.append(exact(group(d_mixed, c), inherit * group(query_dec, c), TN))
    total = pulls[groups - 1]
    through = dec[groups - 1]
    for c in range(groups - 2, -1, -1):
        total = pulls[c] + dec[c] * total
        through = through * dec[c]
    r.chain_send[1, pl.ds(0, DV)] = total.astype(BF16)
    r.chain_send[1, pl.ds(DV, 16)] = lines_of(through)
    chain_start(1)
    rs(UP, 2)
    rs(DOWN, 3)
    value = proj[:, 2 * DK : 2 * DK + DV]
    key_inc = r.key_inc[...]
    ti = lax.broadcasted_iota(jnp.int32, (length, length), 0)
    tj = lax.broadcasted_iota(jnp.int32, (length, length), 1)
    below = jnp.logical_and(ti // GROUP == tj // GROUP, ti >= tj)
    seg_row = r.seg_in[...].astype(F32) + 1.0
    seg_wide = jnp.concatenate([seg_l] * (length // DK), axis=1)
    joined = jnp.logical_and(below, seg_wide == seg_row)
    d_scores = jnp.where(joined, exact(d_mixed, value, NT), 0.0)
    d_value = exact(r.scores[...], d_mixed, TN)
    carried = jnp.concatenate(
        [
            (group(seg_l, c) == before[c]).astype(F32) * exact(group(d_mixed, c), r.states[c], NN)
            for c in range(groups)
        ],
        axis=0,
    )
    d_query_dec = exact(d_scores, key_inc, NN) + carried
    d_key_inc = exact(d_scores, query_dec, TN)
    rs(GATE, 3)
    rs(UP, 3)
    rs(OUT, 1)
    chain_wait(1)
    pull = chain_sum(1)
    key = proj[:, DK : 2 * DK]
    fade = r.fade[...]
    key_final = key * fade
    d_finals, d_values, d_ends = [None] * groups, [None] * groups, [None] * groups
    for c in range(groups - 1, -1, -1):
        d_final = exact(group(value, c), pull, NN)
        d_finals[c] = d_final
        d_values[c] = group(d_value, c) + exact(group(key_final, c), pull, NT)
        d_end = jnp.sum(d_final * group(key_final, c), axis=0, keepdims=True) + dec[c] * jnp.sum(
            r.states[c] * pull, axis=0, keepdims=True
        )
        d_ends[c] = jnp.broadcast_to(d_end, (GROUP, DK))
        pull = pulls[c] + dec[c] * pull
    d_final = jnp.concatenate(d_finals, axis=0)
    r.d_proj[:, 0:DK] = (d_query_dec * grown * scale).astype(BF16)
    r.d_proj[:, DK : 2 * DK] = (d_key_inc * r.shrunk[...] + d_final * fade).astype(BF16)
    r.d_proj[:, 2 * DK : 2 * DK + DV] = jnp.concatenate(d_values, axis=0).astype(BF16)
    d_cumul = d_query_dec * query_dec - d_key_inc * key_inc - d_final * key_final
    above = jnp.logical_and(ti // GROUP == tj // GROUP, ti <= tj)
    d_logdec = exact(above.astype(F32), d_cumul, NN) + jnp.concatenate(d_ends, axis=0)
    logit = r.logit[...]
    d_logit = d_logdec * jax.nn.sigmoid(-logit) / 16.0
    bias_row = jnp.sum(d_logit, axis=0, keepdims=True)
    rank = folded(wd[pl.ds(16, 16), :].astype(F32))
    grad_rank = exact(r.low[...], d_logit, TN)
    d_low = exact(d_logit, rank, NT).astype(BF16)
    d_proj = r.d_proj[...]
    normed = r.normed[...]
    gp[...] = mm(normed, d_proj, TN).astype(BF16).reshape(gp.shape)
    rs(PROJ, 0)
    r.part_i[...] = (
        (mm(d_proj, wp[...], NT) + mm(d_low, wd[pl.ds(0, 16), :], NN))
        .astype(BF16)
        .reshape(r.part_i.shape)
    )
    sum_i[0]()
    rs(DOWN, 4)
    sum_i[1]()
    low_rows = mm(d_low, normed, TN)
    rs(GATE, 4)
    rs(UP, 4)
    rs(OUT, 2)
    rs(PROJ, 1)
    d_normin = sum_i[2]()
    resid_in = r.x_in[...]
    inv_attn = rms_scale(resid_in)
    attn_row = jnp.sum(d_normin * resid_in * inv_attn, axis=0, keepdims=True)
    scaled = gain_attn * d_normin
    r.v_in[...] = (
        r.d_mid[...]
        + inv_attn * scaled
        - resid_in * inv_attn**3 * jnp.mean(scaled * resid_in, axis=-1, keepdims=True)
    )
    emit(r.v_in, r.grad_in)
    gs = r.gs
    gs[...] = jnp.zeros_like(gs)
    for b in range(n):
        cut = slice(b * LANE, (b + 1) * LANE)
        gs[b, 0:16] = low_rows[:, cut]
        gs[b, 16:32] = grad_rank
        gs[b, 32:33] = attn_row[:, cut]
        gs[b, 33:34] = mlp_row[:, cut]
        gs[b, 34:35] = head_row[:, 0:LANE]
        gs[b, 35:36] = head_row[:, LANE : 2 * LANE]
        gs[b, 36:37] = bias_row
    lean = [
        remote(
            gs.at[(s + d) % n],
            r.gs_recv.at[d - 1],
            r.gs_ssem.at[d - 1],
            r.gs_rsem.at[d - 1],
            SHARD,
            (s + d) % n,
        )
        for d in range(1, n)
    ]
    for copy in lean:
        copy.start()
    rs(DOWN, 5)
    rs(GATE, 5)
    rs(UP, 5)
    rs(OUT, 3)
    rs(PROJ, 2)
    mine = gs[s]
    for d, copy in enumerate(lean):
        copy.wait_recv()
        mine = mine + r.gs_recv[d]
    r.lean_send[...] = mine
    heads = [
        remote(
            r.lean_send,
            r.hs_recv.at[d - 1],
            r.hs_ssem.at[d - 1],
            r.hs_rsem.at[d - 1],
            HEAD,
            (me + d) % 4,
        )
        for d in range(1, 4)
    ]
    for copy in heads:
        copy.start()
    rs(DOWN, 6)
    rs(GATE, 6)
    rs(UP, 6)
    rs(OUT, 4)
    rs(PROJ, 3)
    rs_finish(DOWN)
    rs_finish(GATE)
    rs_finish(UP)
    rs(OUT, 5)
    rs(PROJ, 4)
    for d, copy in enumerate(heads):
        copy.wait_recv()
        mine = mine + r.hs_recv[d]
    quarter = LANE // 4
    by_head = pltpu.roll(mine, (LANE - quarter * me) % LANE, 1)
    by_shard = pltpu.roll(r.lean_send[...], (LANE - part_k * s) % LANE, 1)
    gains = pltpu.roll(mine, (2 * LANE - part_v * s - (part_v // 4) * me) % LANE, 1)
    r.lean[0:16] = by_head[0:16]
    r.lean[16:32] = by_shard[16:32]
    r.lean[32:48] = jnp.concatenate(
        [by_head[32:34], jnp.where(lower, gains[34:35], gains[35:36]), by_shard[36:37], by_head[36:48]],
        axis=0,
    )
    emit(r.lean, r.g_lean)
    rs(OUT, 6)
    rs(PROJ, 5)
    rs_finish(OUT)
    rs(PROJ, 6)
    rs_finish(PROJ)
    for copy in lean + heads:
        copy.wait_send()
    for one in (gather_x, gather_c, gather_m, gather_d, sum_o, sum_m, sum_i):
        one[3]()
    chain_drain(0)
    chain_drain(1)
    ag_drain()
    rs_drain()
    for copy in written:
        copy.wait()


def finish_kernel(count, *refs):
    ins, outs = refs[:count], refs[count + 1 : 2 * count + 1]
    lean = refs[count]
    small = refs[2 * count + 1 : 2 * count + 7]
    stage = refs[2 * count + 7 : 3 * count + 7]
    held, rank, low, attn, mlp, head, bias, in_sem, out_sem = refs[3 * count + 7 :]
    first = pltpu.make_async_copy(lean, held, in_sem.at[count])
    first.start()
    there = [pltpu.make_async_copy(a, b, in_sem.at[i]) for i, (a, b) in enumerate(zip(ins, stage))]
    for copy in there:
        copy.start()
    first.wait()
    for i in range(GATE_RANK):
        rank[i] = held[16 + i : 17 + i, 0 : rank.shape[2]]
    low[...] = held[0:16, 0 : low.shape[1]]
    attn[...] = held[32:33, 0 : attn.shape[1]]
    mlp[...] = held[33:34, 0 : mlp.shape[1]]
    head[...] = held[34:35, 0 : head.shape[1]]
    bias[...] = held[35:36, 0 : bias.shape[1]]
    back = [
        pltpu.make_async_copy(a, b, out_sem.at[i])
        for i, (a, b) in enumerate(
            zip(stage + (rank, low, attn, mlp, head, bias), outs + small)
        )
    ]
    for copy in back[count:]:
        copy.start()
    for one, copy in zip(there, back):
        one.wait()
        copy.start()
    for copy in back:
        copy.wait()


def finish(large, lean, n):
    count = len(large)
    shapes = ((GATE_RANK, 1, DK // n), (GATE_RANK, LANE // 4), (1, LANE // 4), (1, LANE // 4), (1, DV // n // 4), (1, DK // n))
    sem = pltpu.SemaphoreType.DMA
    made = pl.pallas_call(
        functools.partial(finish_kernel, count),
        out_shape=tuple(jax.ShapeDtypeStruct(a.shape, F32) for a in large)
        + tuple(jax.ShapeDtypeStruct(a, F32) for a in shapes),
        in_specs=[pl.BlockSpec(memory_space=pl.ANY)] * (count + 1),
        out_specs=tuple([pl.BlockSpec(memory_space=pl.ANY)] * (count + 6)),
        scratch_shapes=[pltpu.VMEM(a.shape, F32) for a in large]
        + [pltpu.VMEM((SMALL, LANE), F32)]
        + [pltpu.VMEM(a, F32) for a in shapes]
        + [sem((count + 1,)), sem((count + 6,))],
        compiler_params=pltpu.CompilerParams(vmem_limit_bytes=60 * 1024 * 1024),
    )(*large, lean)
    return made[:count], made[count:]


def block(args, ident):
    n = lax.axis_size(SHARD)
    ins = Refs(args)
    wide = ins.w_down.shape[0]
    rows = ins.resid_in.shape[0]
    length = ins.segment.shape[1]
    depth = ins.w_query.shape[0]
    groups = length // GROUP
    reach = min(n - 1, (SEQ + length - 2) // length)

    def out(*shape):
        return jax.ShapeDtypeStruct(shape, F32)

    outs = dict(
        resid_out=out(rows, D),
        grad_in=out(rows, D),
        g_query=out(depth, DK),
        g_key=out(depth, DK),
        g_value=out(depth, DV),
        g_outgate=out(depth, DV),
        g_out=out(DV, LANE),
        g_gate=out(wide, LANE),
        g_up=out(wide, LANE),
        g_down=out(wide, LANE),
        g_lean=out(SMALL, LANE),
    )
    across = 2 * DK + 2 * DV
    tall = SMALL + DV + 3 * wide
    vm = pltpu.VMEM
    sem = pltpu.SemaphoreType.DMA
    scratch = dict(
        wp=vm((D, across), BF16),
        wd=vm((tall, D), BF16),
        x4=vm((4, rows, D), F32),
        cot4=vm((4, rows, D), BF16),
        mid4=vm((4, rows, D), BF16),
        dmid4=vm((4, rows, D), BF16),
        normed=vm((length, D), BF16),
        proj=vm((length, across), F32),
        low=vm((length, GATE_RANK), F32),
        logit=vm((length, DK), F32),
        fade=vm((length, DK), F32),
        grown=vm((length, DK), F32),
        shrunk=vm((length, DK), F32),
        seg_l=vm((length, DK), F32),
        query_dec=vm((length, DK), F32),
        key_inc=vm((length, DK), F32),
        scores=vm((length, length), F32),
        mixed=vm((length, DV), F32),
        states=vm((groups, DV, DK), F32),
        prior=vm((8, DK), F32),
        x_in=vm((rows, D), F32),
        cot_in=vm((rows, D), F32),
        seg_in=vm((1, length), jnp.int32),
        s_low=vm((GATE_RANK, LANE), BF16),
        s_rank=vm((GATE_RANK, DK // n), BF16),
        s_attn=vm((1, LANE), BF16),
        s_mlp=vm((1, LANE), BF16),
        s_head=vm((1, DV // n), BF16),
        s_bias=vm((1, DK // n), BF16),
        pad=vm((32, LANE), F32),
        small=vm((SMALL, LANE), BF16),
        v_resid=vm((rows, D), F32),
        v_in=vm((rows, D), F32),
        v_proj=vm((depth, across), F32),
        v_out=vm((DV, LANE), F32),
        v_gate=vm((wide, LANE), F32),
        v_up=vm((wide, LANE), F32),
        v_down=vm((wide, LANE), F32),
        lean=vm((SMALL, LANE), F32),
        gated=vm((length, DV), BF16),
        resid_mid=vm((rows, D), F32),
        d_mid=vm((rows, D), F32),
        gate_pre=vm((wide, length), F32),
        up_pre=vm((wide, length), F32),
        hidden=vm((wide, length), BF16),
        d_gate=vm((wide, length), BF16),
        d_up=vm((wide, length), BF16),
        d_proj=vm((length, across), BF16),
        gm=vm((n, 3 * wide, LANE), BF16),
        go=vm((n, DV, LANE), BF16),
        gp=vm((n, depth, across), BF16),
        gs=vm((n, SMALL, LANE), F32),
        gs_recv=vm((n - 1, SMALL, LANE), F32),
        lean_send=vm((SMALL, LANE), F32),
        hs_recv=vm((3, SMALL, LANE), F32),
        held_m=vm((n - 1, 3 * wide, LANE), BF16),
        held_o=vm((n - 1, DV, LANE), BF16),
        held_p=vm((n - 1, depth, across), BF16),
        chain_send=vm((2, DV + 16, DK), BF16),
        chain_recv=vm((2, reach, DV + 16, DK), BF16),
    )
    for tag, width in (("o", D), ("m", 2 * D), ("i", D)):
        scratch["part_" + tag] = vm((4, rows, width), BF16)
        scratch["near_" + tag] = vm((2, rows, width), BF16)
        scratch["far_" + tag] = vm((rows, width), BF16)
        scratch["total_" + tag] = vm((rows, width), BF16)
    scratch.update(
        ag_send=sem((11, 2, n // 2)),
        ag_recv=sem((11, 2, n // 2)),
        rs_send=sem((12, n - 1)),
        rs_recv=sem((12, n - 1)),
        qg_send=sem((4, 2, 3)),
        qg_recv=sem((4, 2, 3)),
        qs_send=sem((3, 2, 3)),
        qs_recv=sem((3, 2, 3)),
        chain_ssem=sem((2, reach)),
        chain_rsem=sem((2, reach)),
        gs_ssem=sem((n - 1,)),
        gs_rsem=sem((n - 1,)),
        hs_ssem=sem((3,)),
        hs_rsem=sem((3,)),
        own_sem=sem((17,)),
        out_sem=sem((27,)),
    )
    names = tuple(ins) + tuple(outs) + tuple(scratch)
    made = pl.pallas_call(
        functools.partial(block_kernel, n, reach, names),
        out_shape=tuple(outs.values()),
        in_specs=[pl.BlockSpec(memory_space=pl.ANY)] * len(ins),
        out_specs=tuple(pl.BlockSpec(memory_space=pl.ANY) for _ in outs),
        scratch_shapes=list(scratch.values()),
        compiler_params=pltpu.CompilerParams(
            collective_id=ident, has_side_effects=True, vmem_limit_bytes=60 * 1024 * 1024
        ),
    )(*ins.values())
    return Refs(zip(outs, made))


def fused(
    resid_in,
    cotangent,
    segment,
    attn_gain,
    w_query,
    w_key,
    w_value,
    w_outgate,
    w_low,
    w_rank,
    rank_bias,
    head_gain,
    w_out,
    mlp_gain,
    w_gate,
    w_up,
    w_down,
):
    n = lax.axis_size(SHARD)
    got = block(
        dict(
            resid_in=resid_in,
            cotangent=cotangent,
            segment=segment.reshape(1, -1),
            w_query=w_query,
            w_key=w_key,
            w_value=w_value,
            w_outgate=w_outgate,
            w_low=w_low.T,
            w_rank=w_rank[:, 0, :],
            attn_gain=attn_gain.reshape(1, -1),
            mlp_gain=mlp_gain.reshape(1, -1),
            head_gain=head_gain.reshape(1, -1),
            rank_bias=rank_bias,
            w_out=w_out,
            w_gate=w_gate.T,
            w_up=w_up.T,
            w_down=w_down,
        ),
        1,
    )
    names = [k for k in got if k != "g_lean"]
    large, (rank, low, attn, mlp, head, bias) = finish([got[k] for k in names], got.g_lean, n)
    got = Refs(zip(names, large))
    return (
        got.resid_out,
        got.grad_in,
        attn.reshape(-1),
        got.g_query,
        got.g_key,
        got.g_value,
        got.g_outgate,
        low.T,
        rank,
        bias,
        head.reshape(-1),
        got.g_out,
        mlp.reshape(-1),
        got.g_gate.T,
        got.g_up.T,
        got.g_down,
    )


def on_device(*args):
    n = lax.axis_size(SHARD)
    rows = args[4].shape[0]
    if rows == LANE and n % 2 == 0 and lax.axis_size(HEAD) == 4 and DK % n == 0:
        return fused(*args)
    return split_up(*args)


def solution(mesh):
    in_specs = (
        P((SHARD, HEAD), None),
        P((SHARD, HEAD), None),
        P(SHARD),
        P(SHARD),
        P(SHARD, HEAD),
        P(SHARD, HEAD),
        P(SHARD, HEAD),
        P(SHARD, HEAD),
        P(SHARD, None),
        P(None, HEAD, SHARD),
        P(HEAD, SHARD),
        P(SHARD),
        P(HEAD, SHARD),
        P(SHARD),
        P(SHARD, HEAD),
        P(SHARD, HEAD),
        P(HEAD, SHARD),
    )
    out_specs = (
        P((SHARD, HEAD), None),
        P((SHARD, HEAD), None),
        P((SHARD, HEAD)),
        P(SHARD, HEAD),
        P(SHARD, HEAD),
        P(SHARD, HEAD),
        P(SHARD, HEAD),
        P((SHARD, HEAD), None),
        P(None, HEAD, SHARD),
        P(HEAD, SHARD),
        P((SHARD, HEAD)),
        P(HEAD, SHARD),
        P((SHARD, HEAD)),
        P(SHARD, HEAD),
        P(SHARD, HEAD),
        P(HEAD, SHARD),
    )
    return jax.shard_map(
        on_device, mesh=mesh, in_specs=in_specs, out_specs=out_specs, check_vma=False
    )
```

```python
import functools

import jax
import jax.numpy as jnp
from jax import lax
from jax.experimental import pallas as pl
from jax.experimental.pallas import tpu as pltpu
from jax.sharding import PartitionSpec as P

D = 1024
DK = 128
DV = 256
GATE_RANK = 16
GROUP = 64
LANE = 128
SHARD = "shard"
HEAD = "head"
MESH = pl.DeviceIdType.MESH


EPS = 1e-06
HIGH_PRECISION = lax.Precision.HIGHEST


def ring_index(pos, n):
    return jnp.where(pos < n // 2, 2 * pos, 2 * (n - 1 - pos) + 1)


def ring_place(index, n):
    return jnp.where(index % 2 == 0, index // 2, n - 1 - index // 2)


def greet(*pairs):
    barrier = pltpu.get_barrier_semaphore()
    for axis, peer in pairs:
        pl.semaphore_signal(barrier, inc=1, device_id={axis: peer}, device_id_type=MESH)
    pl.semaphore_wait(barrier, len(pairs))


def remote(source, target, send_sem, recv_sem, axis, peer):
    return pltpu.make_async_remote_copy(
        src_ref=source,
        dst_ref=target,
        send_sem=send_sem,
        recv_sem=recv_sem,
        device_id={axis: peer},
        device_id_type=MESH,
    )


def quad(axis):
    me = lax.axis_index(axis)
    return me, me + 1 - 2 * (me % 2), (me + 2) % 4


def cuts(columns, parts):
    lanes = columns // LANE
    sizes = [(lanes // parts + (1 if i < lanes % parts else 0)) * LANE for i in range(parts)]
    starts = [sum(sizes[:i]) for i in range(parts)]
    return list(zip(starts, sizes))


def ring_gather_kernel(n, axis, x_ref, o_ref, own_sem, send_sem, recv_sem):
    right, left = ring_sides(n, axis)
    greet((axis, left), (axis, right))
    ring_gather_body(n, axis, x_ref, o_ref, own_sem, send_sem, recv_sem, None)


def ring_sides(n, axis):
    pos = ring_place(lax.axis_index(axis), n)
    return ring_index((pos + 1) % n, n), ring_index((pos + n - 1) % n, n)


def ring_gather_body(n, axis, x_ref, o_ref, own_sem, send_sem, recv_sem, meanwhile):
    me = lax.axis_index(axis)
    pos = ring_place(me, n)
    right, left = ring_sides(n, axis)
    own = pltpu.make_async_copy(x_ref, o_ref.at[me], own_sem)
    own.start()
    pieces = cuts(x_ref.shape[1], 2)
    steps = n // 2
    sent = {}
    for step in range(steps):
        for part, (start, size) in enumerate(pieces):
            for way in range(2):
                if step == steps - 1 and part != way:
                    continue
                shift = n - step if way == 0 else step
                block = ring_index((pos + shift) % n, n)
                columns = pl.ds(start, size)
                if step > 0:
                    sent[(step - 1, part, way)].wait_recv()
                source = x_ref.at[:, columns] if step == 0 else o_ref.at[block, :, columns]
                copy = pltpu.make_async_remote_copy(
                    src_ref=source,
                    dst_ref=o_ref.at[block, :, columns],
                    send_sem=send_sem.at[step, part, way],
                    recv_sem=recv_sem.at[step, part, way],
                    device_id={axis: right if way == 0 else left},
                    device_id_type=MESH,
                )
                copy.start()
                sent[(step, part, way)] = copy
        if step == 0 and meanwhile is not None:
            meanwhile()
    for (step, part, way), copy in sent.items():
        if (step + 1, part, way) not in sent:
            copy.wait_recv()
    for copy in sent.values():
        copy.wait_send()
    own.wait()


def ring_gather(x, axis, ident):
    n = lax.axis_size(axis)
    return pl.pallas_call(
        functools.partial(ring_gather_kernel, n, axis),
        out_shape=jax.ShapeDtypeStruct((n,) + x.shape, x.dtype),
        in_specs=[pl.BlockSpec(memory_space=pltpu.VMEM)],
        out_specs=pl.BlockSpec(memory_space=pl.ANY),
        scratch_shapes=[
            pltpu.SemaphoreType.DMA,
            pltpu.SemaphoreType.DMA((n // 2, 2, 2)),
            pltpu.SemaphoreType.DMA((n // 2, 2, 2)),
        ],
        compiler_params=pltpu.CompilerParams(collective_id=ident, has_side_effects=True),
    )(x)


def quad_gather_parts(axis, x_ref, o_ref, send_sem, recv_sem):
    me, beside, across = quad(axis)
    half = x_ref.shape[0] // 2
    parts = [pl.ds(0, half), pl.ds(half, half)]
    first = [
        (
            remote(x_ref.at[rows], o_ref.at[me, rows], send_sem.at[i, 0], recv_sem.at[i, 0], axis, across),
            remote(x_ref.at[rows], o_ref.at[me, rows], send_sem.at[i, 1], recv_sem.at[i, 1], axis, beside),
        )
        for i, rows in enumerate(parts)
    ]
    onward = [
        remote(
            o_ref.at[across, rows],
            o_ref.at[across, rows],
            send_sem.at[i, 2],
            recv_sem.at[i, 2],
            axis,
            beside,
        )
        for i, rows in enumerate(parts)
    ]

    def start():
        for far, near in first:
            far.start()
            near.start()
        o_ref[me] = x_ref[...]

    def relay():
        for (far, _), more in zip(first, onward):
            far.wait_recv()
            more.start()

    def finish():
        for (far, near), more in zip(first, onward):
            near.wait_recv()
            more.wait_recv()
            far.wait_send()
            near.wait_send()
            more.wait_send()

    return start, relay, finish


def gather_kernel(axis, x_ref, o_ref, send_sem, recv_sem):
    _, beside, across = quad(axis)
    greet((axis, beside), (axis, across))
    start, relay, finish = quad_gather_parts(axis, x_ref, o_ref, send_sem, recv_sem)
    start()
    relay()
    finish()


def gather(x, axis, ident):
    return pl.pallas_call(
        functools.partial(gather_kernel, axis),
        out_shape=jax.ShapeDtypeStruct((4,) + x.shape, x.dtype),
        in_specs=[pl.BlockSpec(memory_space=pltpu.VMEM)],
        out_specs=pl.BlockSpec(memory_space=pltpu.VMEM),
        scratch_shapes=[
            pltpu.SemaphoreType.DMA((2, 3)),
            pltpu.SemaphoreType.DMA((2, 3)),
        ],
        compiler_params=pltpu.CompilerParams(collective_id=ident, has_side_effects=True),
    )(x)


def enter_kernel(n, w_ref, x_ref, spread_ref, o_ref, own_sem, send_w, recv_w, send_x, recv_x):
    right, left = ring_sides(n, SHARD)
    _, beside, across = quad(HEAD)
    greet((SHARD, left), (SHARD, right), (HEAD, beside), (HEAD, across))
    start, relay, finish = quad_gather_parts(HEAD, x_ref, o_ref, send_x, recv_x)
    start()
    ring_gather_body(n, SHARD, w_ref, spread_ref, own_sem, send_w, recv_w, relay)
    finish()


def enter(weights, x, ident):
    n = lax.axis_size(SHARD)
    return pl.pallas_call(
        functools.partial(enter_kernel, n),
        out_shape=(
            jax.ShapeDtypeStruct((n,) + weights.shape, weights.dtype),
            jax.ShapeDtypeStruct((4,) + x.shape, x.dtype),
        ),
        in_specs=[pl.BlockSpec(memory_space=pltpu.VMEM)] * 2,
        out_specs=(
            pl.BlockSpec(memory_space=pl.ANY),
            pl.BlockSpec(memory_space=pltpu.VMEM),
        ),
        scratch_shapes=[
            pltpu.SemaphoreType.DMA,
            pltpu.SemaphoreType.DMA((n // 2, 2, 2)),
            pltpu.SemaphoreType.DMA((n // 2, 2, 2)),
            pltpu.SemaphoreType.DMA((2, 3)),
            pltpu.SemaphoreType.DMA((2, 3)),
        ],
        compiler_params=pltpu.CompilerParams(collective_id=ident, has_side_effects=True),
    )(weights, x)


def ring_sum_kernel(n, axis, pieces, count, *refs):
    g_refs, o_refs = refs[:count], refs[count : 2 * count]
    held, send_sem, recv_sem = refs[2 * count :]
    me = lax.axis_index(axis)
    pos = ring_place(me, n)
    right, left = ring_sides(n, axis)
    greet((axis, left), (axis, right))

    def slot_of(step, part):
        start, size = pieces[part][3:]
        return held.at[step, :, pl.ds(start, size)]

    def copy_of(step, part, source):
        return remote(
            source,
            slot_of(step, part),
            send_sem.at[step, part],
            recv_sem.at[step, part],
            axis,
            right if pieces[part][1] == 0 else left,
        )

    def own_of(step, part):
        which, way, start, _, size = pieces[part]
        shift = 2 * n - 1 - step if way == 0 else 1 + step
        return g_refs[which].at[ring_index((pos + shift) % n, n), :, pl.ds(start, size)]

    for part in range(len(pieces)):
        copy_of(0, part, own_of(0, part)).start()

    def one(step, carry):
        for part in range(len(pieces)):
            slot = slot_of(step - 1, part)
            copy_of(step - 1, part, slot).wait_recv()
            slot[...] = (
                slot[...].astype(jnp.float32) + own_of(step, part)[...].astype(jnp.float32)
            ).astype(held.dtype)
            copy_of(step, part, slot).start()
        return carry

    lax.fori_loop(1, n - 1, one, 0)
    for part, (which, way, start, _, size) in enumerate(pieces):
        slot = slot_of(n - 2, part)
        copy_of(n - 2, part, slot).wait_recv()
        columns = pl.ds(start, size)
        o_refs[which][:, columns] = slot[...].astype(jnp.float32) + g_refs[which][
            me, :, columns
        ].astype(jnp.float32)

    def drain(step, carry):
        for part in range(len(pieces)):
            copy_of(step, part, slot_of(step, part)).wait_send()
        return carry

    lax.fori_loop(0, n - 1, drain, 0)


def ring_sum(gs, plan, axis, ident):
    n, rows, _ = gs[0].shape
    pieces, at = [], 0
    for which, way, start, size in plan:
        pieces.append((which, way, start, at, size))
        at += size
    return pl.pallas_call(
        functools.partial(ring_sum_kernel, n, axis, tuple(pieces), len(gs)),
        out_shape=tuple(jax.ShapeDtypeStruct(g.shape[1:], jnp.float32) for g in gs),
        in_specs=[pl.BlockSpec(memory_space=pltpu.VMEM)] * len(gs),
        out_specs=tuple(pl.BlockSpec(memory_space=pltpu.VMEM) for _ in gs),
        scratch_shapes=[
            pltpu.VMEM((n - 1, rows, at), gs[0].dtype),
            pltpu.SemaphoreType.DMA((n - 1, len(pieces))),
            pltpu.SemaphoreType.DMA((n - 1, len(pieces))),
        ],
        compiler_params=pltpu.CompilerParams(collective_id=ident, has_side_effects=True),
    )(*gs)


def scatter_sum_kernel(axis, x_ref, o_ref, near, far, total, send_sem, recv_sem):
    me, beside, across = quad(axis)
    greet((axis, beside), (axis, across))
    half = o_ref.shape[0] // 2
    parts = [pl.ds(0, half), pl.ds(half, half)]

    def pair(i, k, chunk):
        return remote(
            x_ref.at[chunk, parts[i]],
            near.at[k, parts[i]],
            send_sem.at[i, k],
            recv_sem.at[i, k],
            axis,
            beside,
        )

    copies = [pair(i, 0, (beside + 2) % 4) for i in range(2)]
    copies += [pair(i, 1, beside) for i in range(2)]
    for copy in copies:
        copy.start()
    crossing = []
    for i, rows in enumerate(parts):
        copies[i].wait_recv()
        total[rows] = (
            x_ref[across, rows].astype(jnp.float32) + near[0, rows].astype(jnp.float32)
        ).astype(total.dtype)
        copy = remote(
            total.at[rows], far.at[rows], send_sem.at[i, 2], recv_sem.at[i, 2], axis, across
        )
        copy.start()
        crossing.append(copy)
    for i, rows in enumerate(parts):
        copies[2 + i].wait_recv()
        crossing[i].wait_recv()
        o_ref[rows] = (
            x_ref[me, rows].astype(jnp.float32)
            + near[1, rows].astype(jnp.float32)
            + far[rows].astype(jnp.float32)
        )
    for copy in copies + crossing:
        copy.wait_send()


def scatter_sum(x, axis, ident):
    rows, columns = x.shape[0] // 4, x.shape[1]
    return pl.pallas_call(
        functools.partial(scatter_sum_kernel, axis),
        out_shape=jax.ShapeDtypeStruct((rows, columns), jnp.float32),
        in_specs=[pl.BlockSpec(memory_space=pltpu.VMEM)],
        out_specs=pl.BlockSpec(memory_space=pltpu.VMEM),
        scratch_shapes=[
            pltpu.VMEM((2, rows, columns), x.dtype),
            pltpu.VMEM((rows, columns), x.dtype),
            pltpu.VMEM((rows, columns), x.dtype),
            pltpu.SemaphoreType.DMA((2, 3)),
            pltpu.SemaphoreType.DMA((2, 3)),
        ],
        compiler_params=pltpu.CompilerParams(collective_id=ident, has_side_effects=True),
    )(x.reshape(4, rows, columns))


def chain(decay, state, first, last, backward, ident):
    n = lax.axis_size(SHARD)
    me = lax.axis_index(SHARD)
    lines = jnp.zeros((16, DV), jnp.float32)
    lines = lines.at[0, :DK].set(decay).at[1, 0].set(first).at[1, 1].set(last)
    block = jnp.concatenate([state, lines], axis=0).astype(jnp.bfloat16)
    every = ring_gather(block, SHARD, ident)
    states = every[:, :DK].astype(jnp.float32)
    decays = every[:, DK, :DK].astype(jnp.float32)
    firsts = every[:, DK + 1, 0].astype(jnp.float32)
    lasts = every[:, DK + 1, 1].astype(jnp.float32)
    place = jnp.arange(n)
    j, i = place[:, None], place[None, :]
    if backward:
        passing = decays
        between = jnp.logical_and(i > me, i < j)
        counted = place > me
    else:
        before = jnp.concatenate([jnp.zeros((1,), jnp.float32), lasts[:-1]])
        passing = decays * (firsts == before).astype(jnp.float32)[:, None]
        between = jnp.logical_and(i > j, i < me)
        counted = place < me
    weight = jnp.prod(jnp.where(between[:, :, None], passing[None], 1.0), axis=1)
    weight = jnp.where(counted[:, None], weight, 0.0)
    incoming = jnp.sum(weight[:, :, None] * states, axis=0)
    prior = jnp.sum(jnp.where(place == me - 1, lasts, 0.0))
    return incoming[None], prior


def rms_scale(values):
    return lax.rsqrt(jnp.mean(values * values, axis=-1, keepdims=True) + EPS)


def running(values):
    place = jnp.arange(values.shape[0])
    below = (place[:, None] >= place[None, :]).astype(jnp.float32)
    return jnp.einsum("ts,shk->thk", below, values, precision=HIGH_PRECISION)


def group_pass(query, key, value_rows, logdec, segf, state, carry_seg):
    total = query.shape[0]
    heads = query.shape[1]
    count = total // GROUP
    scale = DK ** (-0.5)
    order = jnp.arange(GROUP)
    causal = order[:, None] >= order[None, :]

    def blocks(array):
        return array.reshape((count, GROUP) + array.shape[1:])

    def advance(carry, pieces):
        memory_state, prior = carry
        query_c, key_c, value_segment, decay_c, seg_c = pieces
        cumul = running(decay_c)
        query_decayed = query_c * jnp.exp(cumul) * scale
        key_inc = key_c * jnp.exp(-cumul)
        scores = jnp.einsum("thk,shk->hts", query_decayed, key_inc, precision=HIGH_PRECISION)
        joined = jnp.logical_and(causal, seg_c[:, None] == seg_c[None, :])
        scores = jnp.where(joined[None], scores, 0.0)
        inherit = (seg_c == prior).astype(jnp.float32)
        inside = jnp.einsum("hts,shv->thv", scores, value_segment, precision=HIGH_PRECISION)
        carried_state = jnp.einsum(
            "zsb,sbi->zsi", query_decayed, memory_state, precision=HIGH_PRECISION
        )
        result = inside + inherit[:, None, None] * carried_state
        final_result = cumul[-1]
        keep = (seg_c == seg_c[-1]).astype(jnp.float32)
        key_final_rows = key_c * jnp.exp(final_result[None] - cumul) * keep[:, None, None]
        linked_states = (seg_c[-1] == prior).astype(jnp.float32)
        memory_state = linked_states * jnp.exp(final_result)[
            :, :, None
        ] * memory_state + jnp.einsum(
            "zie,zir->ier", key_final_rows, value_segment, precision=HIGH_PRECISION
        )
        return ((memory_state, seg_c[-1]), result)

    (memory_state, last_seg), outs = lax.scan(
        advance,
        (state, carry_seg),
        (blocks(query), blocks(key), blocks(value_rows), blocks(logdec), blocks(segf)),
        unroll=True,
    )
    return (outs.reshape(total, heads, outs.shape[-1]), memory_state)


def split_up(
    resid_in,
    cotangent,
    segment,
    attn_gain,
    w_query,
    w_key,
    w_value,
    w_outgate,
    w_low,
    w_rank,
    rank_bias,
    head_gain,
    w_out,
    mlp_gain,
    w_gate,
    w_up,
    w_down,
):

    n = lax.axis_size(SHARD)
    wide = w_gate.shape[1]
    rows = w_query.shape[0]

    def tall(a):
        a = a.reshape(a.shape[0], -1)
        return jnp.pad(a, ((0, rows - a.shape[0]), (0, 0)))

    packed = jnp.concatenate(
        [
            w_query,
            w_key,
            w_value,
            w_outgate,
            w_out.T,
            w_gate,
            w_up,
            w_down.T,
            w_low,
            tall(attn_gain),
            tall(mlp_gain),
            tall(head_gain),
            tall(w_rank[:, 0, :].T),
            tall(rank_bias[0]),
        ],
        axis=1,
    )
    used = packed.shape[1]
    packed = jnp.pad(packed, ((0, 0), (0, -used % LANE)))
    inv_attn = rms_scale(resid_in)
    unit_rows = (resid_in * inv_attn).astype(jnp.bfloat16)
    cot_rows = cotangent.astype(jnp.bfloat16)
    every, both = enter(packed, jnp.concatenate([unit_rows, cot_rows], axis=1), 1)
    spread = every.reshape(n * rows, packed.shape[1])
    edge_out = 2 * DK + 2 * DV
    edge_gate = edge_out + DV
    edge_down = edge_gate + 2 * wide
    edge_low = edge_down + wide
    project_w = spread[:, :edge_out]
    out_wt = spread[:, edge_out:edge_gate]
    gu_w = spread[:, edge_gate:edge_down]
    down_wt = spread[:, edge_down:edge_low]
    tail = every[:, :, edge_low:]
    low_w = tail[:, :, :GATE_RANK].reshape(D, GATE_RANK)
    gain_attn = tail[:, :, GATE_RANK].reshape(D).astype(jnp.float32)
    gain_mlp = tail[:, :, GATE_RANK + 1].reshape(D).astype(jnp.float32)
    gain_head = tail[:, : DV // n, GATE_RANK + 2].reshape(DV).astype(jnp.float32)
    rank_w = tail[:, : DK // n, GATE_RANK + 3 : 2 * GATE_RANK + 3].reshape(DK, GATE_RANK).T
    bias_w = tail[:, : DK // n, 2 * GATE_RANK + 3].reshape(DK)
    length = segment.shape[0]
    local_heads = 1
    scale = DK ** (-0.5)
    normed_in = (
        (both[:, :, :D].astype(jnp.float32) * gain_attn).astype(jnp.bfloat16).reshape(length, D)
    )
    cot_bf = both[:, :, D:].reshape(length, D)
    projected = jnp.dot(normed_in, project_w, preferred_element_type=jnp.float32)
    query = projected[:, :DK].reshape(length, local_heads, DK)
    key = projected[:, DK : 2 * DK].reshape(length, local_heads, DK)
    value_rows = projected[:, 2 * DK : 2 * DK + DV].reshape(length, local_heads, DV)
    outgate = projected[:, 2 * DK + DV :].reshape(length, local_heads, DV)
    low = jnp.dot(normed_in, low_w, preferred_element_type=jnp.float32)
    rank_mat = rank_w.astype(jnp.float32).reshape(GATE_RANK, local_heads * DK)
    logit = jnp.dot(low, rank_mat, precision=HIGH_PRECISION) + bias_w.astype(jnp.float32).reshape(
        local_heads * DK
    )
    logdec = (jax.nn.log_sigmoid(logit) / 16.0).reshape(length, local_heads, DK)
    segf = segment.astype(jnp.float32) + 1.0
    first_seg = segf[:1]
    last_seg = segf[-1:]
    cumul = running(logdec)
    keep = (segf == last_seg[0]).astype(jnp.float32)
    key_final_rows = key * jnp.exp(cumul[-1][None] - cumul) * keep[:, None, None]
    summary_state = jnp.einsum("zie,zir->ier", key_final_rows, value_rows, precision=HIGH_PRECISION)
    through = jnp.exp(cumul[-1]) * (first_seg[0] == last_seg[0]).astype(jnp.float32)
    state_in, prior = chain(through[0], summary_state[0], first_seg[0], last_seg[0], False, 3)

    def mixer(query_in, key_in, value_in, decay_in):
        return group_pass(query_in, key_in, value_in, decay_in, segf, state_in, prior)

    (mixed, state_out), mixer_back = jax.vjp(mixer, query, key, value_rows, logdec)
    inv_head = rms_scale(mixed)
    headnormed = mixed * inv_head * gain_head
    sigma_out = jax.nn.sigmoid(outgate)
    swish_out = outgate * sigma_out
    gated = (headnormed * swish_out).reshape(length, local_heads * DV).astype(jnp.bfloat16)
    resid_mid = resid_in + scatter_sum(
        jnp.dot(gated, out_wt.T, preferred_element_type=jnp.float32).astype(jnp.bfloat16),
        HEAD,
        4,
    )
    inv_mlp = rms_scale(resid_mid)
    mid_rows = (resid_mid * inv_mlp * gain_mlp).astype(jnp.bfloat16)
    normed_mid = gather(mid_rows, HEAD, 5).reshape(length, D)
    gate_up = jnp.dot(normed_mid, gu_w, preferred_element_type=jnp.float32)
    gate_pre = gate_up[:, :wide]
    up_pre = gate_up[:, wide:]
    sigma_gate = jax.nn.sigmoid(gate_pre)
    active = gate_pre * sigma_gate
    hidden = (active * up_pre).astype(jnp.bfloat16)
    d_hidden = jnp.dot(cot_bf, down_wt, preferred_element_type=jnp.float32)
    d_gatepre = (d_hidden * up_pre * sigma_gate * (1.0 + gate_pre * (1.0 - sigma_gate))).astype(
        jnp.bfloat16
    )
    d_uppre = (d_hidden * active).astype(jnp.bfloat16)
    d_gu = jnp.concatenate([d_gatepre, d_uppre], axis=1)
    grad_down = jnp.dot(cot_bf.T, hidden, preferred_element_type=jnp.float32)
    grad_gu = jnp.dot(normed_mid.T, d_gu, preferred_element_type=jnp.float32)
    shares = jnp.concatenate(
        [
            jnp.dot(hidden, down_wt.T, preferred_element_type=jnp.float32).astype(jnp.bfloat16),
            jnp.dot(d_gu, gu_w.T, preferred_element_type=jnp.float32).astype(jnp.bfloat16),
        ],
        axis=1,
    )
    summed = scatter_sum(shares, HEAD, 6)
    resid_out = resid_mid + summed[:, :D]
    d_normmid = summed[:, D:]
    part_mlp_gain = jnp.sum(d_normmid * resid_mid * inv_mlp, axis=0)
    scaled_mid = gain_mlp * d_normmid
    d_mid = (
        cotangent
        + inv_mlp * scaled_mid
        - resid_mid * inv_mlp**3 * jnp.mean(scaled_mid * resid_mid, axis=-1, keepdims=True)
    )
    dmid_rows = d_mid.astype(jnp.bfloat16)
    dmid_bf = gather(dmid_rows, HEAD, 7).reshape(length, D)
    d_gated = jnp.dot(dmid_bf, out_wt, preferred_element_type=jnp.float32).reshape(
        length, local_heads, DV
    )
    grad_out = jnp.dot(dmid_bf.T, gated, preferred_element_type=jnp.float32)
    d_head = d_gated * swish_out
    d_outgate = (
        (d_gated * headnormed * sigma_out * (1.0 + outgate * (1.0 - sigma_out)))
        .reshape(length, local_heads * DV)
        .astype(jnp.bfloat16)
    )
    part_head_gain = jnp.sum(d_head * mixed * inv_head, axis=(0, 1))
    scaled_head = gain_head * d_head
    mixed_gradient = inv_head * scaled_head - mixed * inv_head**3 * jnp.mean(
        scaled_head * mixed, axis=-1, keepdims=True
    )
    inherit = (segf == prior).astype(jnp.float32)
    weighted_query = query * jnp.exp(cumul) * inherit[:, None, None] * scale
    local_gradient = jnp.einsum(
        "zie,zir->ier", weighted_query, mixed_gradient, precision=HIGH_PRECISION
    )
    through_all = jnp.exp(cumul[-1]) * (last_seg[0] == prior).astype(jnp.float32)
    nothing = jnp.zeros((), jnp.float32)
    outgoing, _ = chain(through_all[0], local_gradient[0], nothing, nothing, True, 8)
    d_query, d_key, d_value, d_logdec = mixer_back((mixed_gradient, outgoing))
    query_bf = d_query.reshape(length, local_heads * DK).astype(jnp.bfloat16)
    key_bf = d_key.reshape(length, local_heads * DK).astype(jnp.bfloat16)
    value_bf = d_value.reshape(length, local_heads * DV).astype(jnp.bfloat16)
    d_logit = d_logdec.reshape(length, local_heads * DK) * jax.nn.sigmoid(-logit) / 16.0
    grad_bias = jnp.sum(d_logit, axis=0).reshape(local_heads, DK)
    grad_rank = jnp.dot(low.T, d_logit, precision=HIGH_PRECISION).reshape(
        GATE_RANK, local_heads, DK
    )
    d_low = (
        jnp.einsum(
            "thk,rhk->thr",
            d_logit.reshape(length, local_heads, DK),
            rank_w.astype(jnp.float32).reshape(GATE_RANK, local_heads, DK),
            precision=HIGH_PRECISION,
        )
        .astype(jnp.bfloat16)
        .reshape(length, local_heads * GATE_RANK)
    )
    part_low = (
        jnp.dot(normed_in.T, d_low, preferred_element_type=jnp.float32)
        .reshape(D, local_heads, GATE_RANK)
        .sum(axis=1)
    )
    d_project = jnp.concatenate([query_bf, key_bf, value_bf, d_outgate], axis=1)
    grad_project = jnp.dot(normed_in.T, d_project, preferred_element_type=jnp.float32)
    low_rows = low_w.T
    total_term = jnp.dot(d_project, project_w.T, preferred_element_type=jnp.float32)
    d_normin = scatter_sum(
        (total_term + jnp.dot(d_low, low_rows, preferred_element_type=jnp.float32)).astype(
            jnp.bfloat16
        ),
        HEAD,
        9,
    )
    part_attn_gain = jnp.sum(d_normin * resid_in * inv_attn, axis=0)
    scaled_in = gain_attn * d_normin
    grad_in = (
        d_mid
        + inv_attn * scaled_in
        - resid_in * inv_attn**3 * jnp.mean(scaled_in * resid_in, axis=-1, keepdims=True)
    )

    def owners(a):
        a = a.reshape(n, a.shape[0] // n, -1)
        return jnp.pad(a, ((0, 0), (0, rows - a.shape[1]), (0, 0))).reshape(D, -1)

    lean = jnp.concatenate(
        [
            part_low,
            part_attn_gain[:, None],
            part_mlp_gain[:, None],
            owners(part_head_gain),
            owners(grad_rank[:, 0, :].T),
            owners(grad_bias[0]),
        ],
        axis=1,
    )
    lean = jnp.pad(lean, ((0, 0), (0, packed.shape[1] - used)))
    grads = [
        g.astype(jnp.bfloat16).reshape(n, rows, -1)
        for g in (
            grad_project,
            grad_out,
            grad_gu,
            jnp.concatenate([grad_down, lean], axis=1),
        )
    ]
    middle = (wide // LANE + 1) * LANE
    plan = (
        (2, 0, 0, middle),
        (3, 1, 0, grads[3].shape[2]),
        (0, 0, 0, edge_out),
        (2, 1, middle, 2 * wide - middle),
        (1, 1, 0, DV),
    )
    own_project, own_out, own_gu, own_rest = ring_sum(grads, plan, SHARD, 10)
    heads = lax.axis_size(HEAD)
    shared = own_rest[:, wide : wide + GATE_RANK + 3]
    gain_rows = DV // n
    final_rank = own_rest[: DK // n, wide + GATE_RANK + 3 : wide + 2 * GATE_RANK + 3]
    final_bias = own_rest[: DK // n, wide + 2 * GATE_RANK + 3]
    shares = jnp.concatenate(
        [
            shared[:, : GATE_RANK + 2].reshape(heads, rows // heads, GATE_RANK + 2),
            jnp.pad(
                shared[:gain_rows, GATE_RANK + 2].reshape(heads, gain_rows // heads, 1),
                ((0, 0), (0, (rows - gain_rows) // heads), (0, 0)),
            ),
        ],
        axis=2,
    )
    deep = max(rows // heads, 32)
    shares = jnp.pad(
        shares, ((0, 0), (0, deep - rows // heads), (0, LANE - GATE_RANK - 3))
    ).reshape(heads * deep, LANE)
    final = scatter_sum(shares.astype(jnp.bfloat16), HEAD, 11)[: rows // heads]
    return (
        resid_out,
        grad_in,
        final[:, GATE_RANK],
        own_project[:, :DK],
        own_project[:, DK : 2 * DK],
        own_project[:, 2 * DK : 2 * DK + DV],
        own_project[:, 2 * DK + DV :],
        final[:, :GATE_RANK],
        final_rank.T.reshape(GATE_RANK, 1, DK // n),
        final_bias.reshape(1, DK // n),
        final[: gain_rows // heads, GATE_RANK + 2],
        own_out.T,
        final[:, GATE_RANK + 1],
        own_gu[:, :wide],
        own_gu[:, wide:],
        own_rest[:, :wide].T,
    )


SEQ = 1024
NN = ((1,), (0,))
NT = ((1,), (1,))
TN = ((0,), (0,))
SMALL = 48
F32 = jnp.float32
BF16 = jnp.bfloat16


def mm(a, b, dims, precision=None):
    return lax.dot_general(
        a, b, (dims, ((), ())), precision=precision, preferred_element_type=F32
    )


def exact(a, b, dims):
    return mm(a, b, dims, HIGH_PRECISION)


def quad_gather(buf, send_sem, recv_sem):
    me, beside, across = quad(HEAD)
    half = buf.shape[1] // 2
    first, onward = [], []
    for i in range(2):
        rows = pl.ds(i * half, half)
        own, got = buf.at[me, rows], buf.at[across, rows]
        far = remote(own, own, send_sem.at[i, 0], recv_sem.at[i, 0], HEAD, across)
        near = remote(own, own, send_sem.at[i, 1], recv_sem.at[i, 1], HEAD, beside)
        more = remote(got, got, send_sem.at[i, 2], recv_sem.at[i, 2], HEAD, beside)
        first.append((far, near))
        onward.append(more)

    def start():
        for far, near in first:
            far.start()
            near.start()

    def relay():
        for (far, _), more in zip(first, onward):
            far.wait_recv()
            more.start()

    def finish():
        for (_, near), more in zip(first, onward):
            near.wait_recv()
            more.wait_recv()

    def drain():
        for (far, near), more in zip(first, onward):
            far.wait_send()
            near.wait_send()
            more.wait_send()

    return start, relay, finish, drain


def quad_sum(part, near, far, total, send_sem, recv_sem):
    me, beside, across = quad(HEAD)
    half = part.shape[1] // 2
    parts = [pl.ds(i * half, half) for i in range(2)]

    def pair(i, k, chunk):
        return remote(
            part.at[chunk, parts[i]],
            near.at[k, parts[i]],
            send_sem.at[i, k],
            recv_sem.at[i, k],
            HEAD,
            beside,
        )

    copies = [pair(i, 0, (beside + 2) % 4) for i in range(2)]
    copies += [pair(i, 1, beside) for i in range(2)]
    crossing = [
        remote(total.at[rows], far.at[rows], send_sem.at[i, 2], recv_sem.at[i, 2], HEAD, across)
        for i, rows in enumerate(parts)
    ]

    def start():
        for copy in copies:
            copy.start()

    def cross():
        for i, rows in enumerate(parts):
            copies[i].wait_recv()
            total[rows] = (part[across, rows].astype(F32) + near[0, rows].astype(F32)).astype(BF16)
            crossing[i].start()

    def finish():
        for i in range(2):
            copies[2 + i].wait_recv()
            crossing[i].wait_recv()
        return part[me].astype(F32) + near[1].astype(F32) + far[...].astype(F32)

    def drain():
        for copy in copies + crossing:
            copy.wait_send()

    return start, cross, finish, drain


class Refs(dict):
    __getattr__ = dict.__getitem__


def block_kernel(n, reach, names, *refs):
    r = Refs(zip(names, refs))
    s = lax.axis_index(SHARD)
    me = lax.axis_index(HEAD)
    _, beside, across = quad(HEAD)
    opposite = (beside + 2) % 4
    pos = ring_place(s, n)
    right, left = ring_sides(n, SHARD)
    steps = n // 2
    wide = r.w_down.shape[0]
    part = wide // 2
    length = r.segment.shape[1]
    groups = length // GROUP
    wp, wd = r.wp, r.wd
    at_out = SMALL
    at_gate = at_out + DV
    at_up = at_gate + wide
    at_down = at_up + wide
    depth = wp.shape[0] // n

    def lanes(b):
        return pl.ds(pl.multiple_of(b * LANE, LANE), LANE)

    def rows_of(b, start, size):
        return pl.ds(pl.multiple_of(b * depth + start, 16), size)

    ag_pieces = []

    def add_rows(start, size, last):
        ag_pieces.append((None, lambda b: wp.at[rows_of(b, start, size)], last))

    def add_lanes(ref, start, size, at, last):
        ag_pieces.append(
            (ref.at[pl.ds(start, size)], lambda b: wd.at[pl.ds(at + start, size), lanes(b)], last)
        )

    add_rows(0, depth // 2, 0)
    add_rows(depth // 2, depth // 2, 1)
    add_lanes(r.small, 0, SMALL, 0, 0)
    add_lanes(r.w_out, 0, DV // 2, at_out, 0)
    add_lanes(r.w_out, DV // 2, DV // 2, at_out, 1)
    add_lanes(r.w_gate, 0, part, at_gate, 0)
    add_lanes(r.w_gate, part, part, at_gate, 1)
    add_lanes(r.w_up, 0, part, at_up, 0)
    add_lanes(r.w_up, part, part, at_up, 1)
    add_lanes(r.w_down, 0, part, at_down, 0)
    add_lanes(r.w_down, part, part, at_down, 1)

    def ag_copy(p, step, way):
        own, place, _ = ag_pieces[p]
        shift = n - step if way == 0 else step
        b = ring_index((pos + shift) % n, n)
        source = own if step == 0 and own is not None else place(b)
        return remote(
            source,
            place(b),
            r.ag_send.at[p, way, step],
            r.ag_recv.at[p, way, step],
            SHARD,
            right if way == 0 else left,
        )

    def ag_has(p, step, way):
        return step < steps - 1 or ag_pieces[p][2] == way

    def ag(ps, step):
        for p in ps:
            for way in range(2):
                if ag_has(p, step, way):
                    if step > 0:
                        ag_copy(p, step - 1, way).wait_recv()
                    ag_copy(p, step, way).start()

    def ag_finish(ps):
        for p in ps:
            for way in range(2):
                if ag_has(p, steps - 1, way):
                    ag_copy(p, steps - 1, way).wait_recv()
                else:
                    ag_copy(p, steps - 2, way).wait_recv()

    def ag_drain():
        for p in range(len(ag_pieces)):
            for step in range(steps):
                for way in range(2):
                    if ag_has(p, step, way):
                        ag_copy(p, step, way).wait_send()

    gm, go, gp = r.gm, r.go, r.gp
    rs_pieces = []
    for start, out in ((0, (r.v_down, r.g_down)), (wide, (r.v_gate, r.g_gate)), (2 * wide, (r.v_up, r.g_up))):
        for way in range(2):
            rs_pieces.append((gm, r.held_m, start + way * part, part, way, (out, way * part)))
    for way in range(2):
        rs_pieces.append((go, r.held_o, way * (DV // 2), DV // 2, way, ((r.v_out, r.g_out), way * (DV // 2))))
    for i in range(4):
        q = depth // 4
        rs_pieces.append((gp, r.held_p, i * q, q, i % 2, ((r.v_proj, None), i * q)))
    DOWN, GATE, UP, OUT, PROJ = (0, 1), (2, 3), (4, 5), (6, 7), (8, 9, 10, 11)

    def rs_own(p, step):
        g, _, start, size, way, _ = rs_pieces[p]
        shift = 2 * n - 1 - step if way == 0 else 1 + step
        return g.at[ring_index((pos + shift) % n, n), pl.ds(start, size)]

    def rs_slot(p, step):
        _, held, start, size, _, _ = rs_pieces[p]
        return held.at[step, pl.ds(start, size)]

    def rs_copy(p, step):
        source = rs_own(p, 0) if step == 0 else rs_slot(p, step - 1)
        return remote(
            source,
            rs_slot(p, step),
            r.rs_send.at[p, step],
            r.rs_recv.at[p, step],
            SHARD,
            right if rs_pieces[p][4] == 0 else left,
        )

    def rs(ps, step):
        for p in ps:
            if step > 0:
                rs_copy(p, step - 1).wait_recv()
                slot = rs_slot(p, step - 1)
                slot[...] = (slot[...].astype(F32) + rs_own(p, step)[...].astype(F32)).astype(BF16)
            rs_copy(p, step).start()

    written = []

    def emit(source, target):
        copy = pltpu.make_async_copy(source, target, r.out_sem.at[len(written)])
        copy.start()
        written.append(copy)

    def rs_finish(ps):
        for p in ps:
            rs_copy(p, n - 2).wait_recv()
            total = rs_slot(p, n - 2)[...].astype(F32) + rs_own(p, n - 1)[...].astype(F32)
            (held, out), start = rs_pieces[p][5]
            rows = pl.ds(start, rs_pieces[p][3])
            held[rows, :] = total
            if out is not None:
                emit(held.at[rows], out.at[rows])
            else:
                at = 0
                for out, width in ((r.g_query, DK), (r.g_key, DK), (r.g_value, DV), (r.g_outgate, DV)):
                    emit(held.at[rows, pl.ds(at, width)], out.at[rows])
                    at += width

    def rs_drain():
        for p in range(len(rs_pieces)):
            for step in range(n - 1):
                rs_copy(p, step).wait_send()

    def chain_copy(which, d):
        send, got = r.chain_send, r.chain_recv
        peer = s + d if which == 0 else s - d
        return remote(
            send.at[which],
            got.at[which, d - 1],
            r.chain_ssem.at[which, d - 1],
            r.chain_rsem.at[which, d - 1],
            SHARD,
            peer,
        )

    def has_peer(which, d):
        return s + d < n if which == 0 else s - d >= 0

    def chain_start(which):
        for d in range(1, reach + 1):
            pl.when(has_peer(which, d))(lambda d=d: chain_copy(which, d).start())

    def chain_wait(which):
        for d in range(1, reach + 1):
            pl.when(has_peer(1 - which, d))(lambda d=d: chain_copy(which, d).wait_recv())

    def chain_drain(which):
        for d in range(1, reach + 1):
            pl.when(has_peer(which, d))(lambda d=d: chain_copy(which, d).wait_send())

    def chain_sum(which):
        got = r.chain_recv
        total = got[which, 0, pl.ds(0, DV)].astype(F32)
        weight = None
        for d in range(2, reach + 1):
            lines = got[which, d - 2, pl.ds(DV, 16)].astype(F32)
            link = lines[0:1]
            if which == 0:
                before = got[which, d - 1, pl.ds(DV, 16)].astype(F32)[2:3]
                link = link * (lines[1:2] == before).astype(F32)
            weight = link if weight is None else weight * link
            total = total + weight * got[which, d - 1, pl.ds(0, DV)].astype(F32)
        return total

    def lines_of(*rows):
        rows = list(rows) + [jnp.zeros((16 - len(rows), DK), F32)]
        return jnp.concatenate(rows, axis=0).astype(BF16)

    gather_x = quad_gather(r.x4, r.qg_send.at[0], r.qg_recv.at[0])
    gather_c = quad_gather(r.cot4, r.qg_send.at[1], r.qg_recv.at[1])
    gather_m = quad_gather(r.mid4, r.qg_send.at[2], r.qg_recv.at[2])
    gather_d = quad_gather(r.dmid4, r.qg_send.at[3], r.qg_recv.at[3])

    def summing(i, tag):
        return quad_sum(
            r["part_" + tag],
            r["near_" + tag],
            r["far_" + tag],
            r["total_" + tag],
            r.qs_send.at[i],
            r.qs_recv.at[i],
        )

    sum_o, sum_m, sum_i = summing(0, "o"), summing(1, "m"), summing(2, "i")

    own_lanes = lanes(s)
    own_rows = rows_of(s, 0, depth)
    moves = [
        (r.resid_in, r.x_in),
        (r.w_low, r.s_low),
        (r.w_rank, r.s_rank),
        (r.attn_gain, r.s_attn),
        (r.mlp_gain, r.s_mlp),
        (r.head_gain, r.s_head),
        (r.rank_bias, r.s_bias),
        (r.w_query, wp.at[own_rows, pl.ds(0, DK)]),
        (r.w_key, wp.at[own_rows, pl.ds(DK, DK)]),
        (r.w_value, wp.at[own_rows, pl.ds(2 * DK, DV)]),
        (r.w_outgate, wp.at[own_rows, pl.ds(2 * DK + DV, DV)]),
        (r.cotangent, r.cot_in),
        (r.segment, r.seg_in),
        (r.w_out, wd.at[pl.ds(at_out, DV), own_lanes]),
        (r.w_gate, wd.at[pl.ds(at_gate, wide), own_lanes]),
        (r.w_up, wd.at[pl.ds(at_up, wide), own_lanes]),
        (r.w_down, wd.at[pl.ds(at_down, wide), own_lanes]),
    ]
    own = [pltpu.make_async_copy(a, b, r.own_sem.at[i]) for i, (a, b) in enumerate(moves)]
    for copy in own:
        copy.start()
    barrier = pltpu.get_barrier_semaphore()
    r.chain_recv[...] = jnp.zeros_like(r.chain_recv)
    for d in range(1, n):
        pl.semaphore_signal(barrier, inc=1, device_id={SHARD: (s + d) % n}, device_id_type=MESH)
    for peer in (beside, across, opposite):
        pl.semaphore_signal(barrier, inc=1, device_id={HEAD: peer}, device_id_type=MESH)
    own[0].wait()
    inv_attn = rms_scale(r.x_in[...])
    r.x4[me] = r.x_in[...] * inv_attn
    for copy in own[1:11]:
        copy.wait()
    part_k, part_v = DK // n, DV // n
    pad = r.pad
    pad[...] = jnp.zeros_like(pad)
    pad[0:GATE_RANK, 0:part_k] = r.s_rank[...].astype(F32)
    pad[16:17, 0:part_k] = r.s_bias[...].astype(F32)
    pad[24:25, 0:part_v] = r.s_head[...].astype(F32)
    by_k = pltpu.roll(pad[0:24], s * part_k, 1)
    by_v = pltpu.roll(pad[24:32], (s * part_v) % LANE, 1)[0:1]
    lower = (lax.broadcasted_iota(jnp.int32, (1, LANE), 1) * 0 + s) < n // 2
    r.small[0:16] = r.s_low[...]
    r.small[16:32] = by_k[0:16].astype(BF16)
    r.small[32:48] = jnp.concatenate(
        [
            r.s_attn[...].astype(F32),
            r.s_mlp[...].astype(F32),
            jnp.where(lower, by_v, 0.0),
            jnp.where(lower, 0.0, by_v),
            by_k[16:17],
            jnp.zeros((11, LANE), F32),
        ],
        axis=0,
    ).astype(BF16)
    wd[pl.ds(0, SMALL), own_lanes] = r.small[...]
    pl.semaphore_wait(barrier, n + 2)

    P0, WO, GU, DN = (0, 1, 2), (3, 4), (5, 6, 7, 8), (9, 10)
    ag(P0, 0)
    gather_x[0]()
    own[11].wait()
    r.cot4[me] = r.cot_in[...].astype(BF16)
    ag(WO, 0)
    gather_x[1]()
    ag(P0, 1)
    gather_c[0]()
    ag(P0, 2)
    ag(WO, 1)
    ag(P0, 3)
    ag(GU, 0)
    gather_x[2]()
    gather_c[1]()
    for copy in own[12:]:
        copy.wait()
    ag_finish(P0)

    fine = wd[pl.ds(32, 16), :].astype(F32)
    gain_attn, gain_mlp = fine[0:1], fine[1:2]

    def folded(block):
        total = block[:, 0:LANE]
        for b in range(1, n):
            total = total + block[:, b * LANE : (b + 1) * LANE]
        return total

    tiny = folded(fine)
    gain_head = jnp.concatenate([tiny[2:3], tiny[3:4]], axis=1)
    bias = tiny[4:5]
    rank = folded(wd[pl.ds(16, 16), :].astype(F32))
    normed = (r.x4[...].reshape(length, D) * gain_attn).astype(BF16)
    r.normed[...] = normed
    proj = r.proj
    low = mm(normed, wd[pl.ds(0, 16), :], NT)
    r.low[...] = low
    logit = exact(low, rank, NN) + bias
    r.logit[...] = logit
    proj[:, 0 : 2 * DK + DV] = mm(normed, wp[:, 0 : 2 * DK + DV], NN)
    logdec = (jnp.minimum(logit, 0.0) - jnp.log1p(jnp.exp(-jnp.abs(logit)))) / 16.0
    ti = lax.broadcasted_iota(jnp.int32, (length, length), 0)
    tj = lax.broadcasted_iota(jnp.int32, (length, length), 1)
    below = jnp.logical_and(ti // GROUP == tj // GROUP, ti >= tj)
    cumul = exact(below.astype(F32), logdec, NN)
    seg_row = r.seg_in[...].astype(F32) + 1.0
    seg_l = jnp.broadcast_to(seg_row, (DK, length)).T
    seg_wide = jnp.concatenate([seg_l] * (length // DK), axis=1)
    joined = jnp.logical_and(below, seg_wide == seg_row)
    scale = DK ** (-0.5)
    query, key = proj[:, 0:DK], proj[:, DK : 2 * DK]
    value = proj[:, 2 * DK : 2 * DK + DV]

    def group(a, c):
        return a[c * GROUP : (c + 1) * GROUP]

    ends = [cumul[(c + 1) * GROUP - 1 : (c + 1) * GROUP] for c in range(groups)]
    last_seg = [seg_l[(c + 1) * GROUP - 1 : (c + 1) * GROUP] for c in range(groups)]
    fade = jnp.concatenate(
        [
            jnp.exp(ends[c] - group(cumul, c)) * (group(seg_l, c) == last_seg[c]).astype(F32)
            for c in range(groups)
        ],
        axis=0,
    )
    key_final = key * fade
    dec = [jnp.exp(e) for e in ends]
    local = [None]
    for c in range(groups):
        update = exact(group(value, c), group(key_final, c), TN)
        if c > 0:
            linked = dec[c] * (last_seg[c] == last_seg[c - 1]).astype(F32)
            update = update + linked * local[c]
        local.append(update)
    whole_end = ends[0]
    for e in ends[1:]:
        whole_end = whole_end + e
    first_seg, final_seg = seg_l[0:1], last_seg[-1]
    through = jnp.exp(whole_end) * (first_seg == final_seg).astype(F32)
    r.chain_send[0, pl.ds(0, DV)] = local[groups].astype(BF16)
    r.chain_send[0, pl.ds(DV, 16)] = lines_of(through, first_seg, final_seg)
    chain_start(0)
    ag(WO, 2)
    ag(WO, 3)
    for c in range(1, groups):
        r.states[c] = local[c]
    r.fade[...] = fade
    r.seg_l[...] = seg_l
    grown = jnp.exp(cumul)
    r.grown[...] = grown
    query_dec = query * grown * scale
    shrunk = jnp.exp(-cumul)
    r.shrunk[...] = shrunk
    key_inc = key * shrunk
    r.query_dec[...] = query_dec
    r.key_inc[...] = key_inc
    scores = jnp.where(joined, exact(query_dec, key_inc, NT), 0.0)
    r.scores[...] = scores
    ag(GU, 1)
    inside = exact(scores, value, NN)
    r.mixed[...] = inside
    outgate = mm(r.normed[...], wp[:, 2 * DK + DV : 2 * DK + 2 * DV], NN)
    proj[:, 2 * DK + DV : 2 * DK + 2 * DV] = outgate
    chain_wait(0)
    state_in = chain_sum(0)
    prior = r.chain_recv[0, 0, pl.ds(DV, 16)].astype(F32)[2:3]
    before = [prior] + last_seg[:-1]
    r.prior[...] = jnp.broadcast_to(prior, (8, DK))
    decay = jnp.ones((1, DK), F32)
    for c in range(groups):
        if c == 0:
            state = state_in
        else:
            decay = decay * dec[c - 1]
            state = r.states[c] + decay * (last_seg[c - 1] == prior).astype(F32) * state_in
        r.states[c] = state
        inherit = (group(seg_l, c) == before[c]).astype(F32)
        r.mixed[pl.ds(c * GROUP, GROUP)] += exact(inherit * group(query_dec, c), state, NT)
    mixed = r.mixed[...]
    inv_head = rms_scale(mixed)
    gated = (mixed * inv_head * gain_head * (outgate * jax.nn.sigmoid(outgate))).astype(BF16)
    r.gated[...] = gated
    ag(GU, 2)
    ag_finish(WO)
    r.part_o[...] = (
        mm(gated, wd[pl.ds(at_out, DV), :], NN).astype(BF16).reshape(r.part_o.shape)
    )
    sum_o[0]()
    ag(DN, 0)
    sum_o[1]()
    gather_c[2]()
    resid_mid = r.x_in[...] + sum_o[2]()
    r.resid_mid[...] = resid_mid
    inv_mlp = rms_scale(resid_mid)
    r.mid4[me] = (resid_mid * inv_mlp * gain_mlp).astype(BF16)
    gather_m[0]()
    ag(GU, 3)
    gather_m[1]()
    ag(DN, 1)
    gather_m[2]()
    ag_finish(GU)

    normed_mid = r.mid4[...].reshape(length, D)
    cot_bf = r.cot4[...].reshape(length, D)
    r.gate_pre[...] = mm(wd[pl.ds(at_gate, wide), :], normed_mid, NT)
    ag(DN, 2)
    r.up_pre[...] = mm(wd[pl.ds(at_up, wide), :], normed_mid, NT)
    gate_pre = r.gate_pre[...]
    r.hidden[...] = (gate_pre * jax.nn.sigmoid(gate_pre) * r.up_pre[...]).astype(BF16)
    ag(DN, 3)

    def spread(g, at, size, value):
        for b in range(n):
            g[b, pl.ds(at, size)] = value[:, b * LANE : (b + 1) * LANE].astype(BF16)

    spread(gm, 0, wide, mm(r.hidden[...], cot_bf, NN))
    rs(DOWN, 0)
    ag_finish(DN)
    d_hidden = mm(wd[pl.ds(at_down, wide), :], cot_bf, NT)
    gate_pre, up_pre = r.gate_pre[...], r.up_pre[...]
    sigma = jax.nn.sigmoid(gate_pre)
    r.d_gate[...] = (d_hidden * up_pre * sigma * (1.0 + gate_pre * (1.0 - sigma))).astype(BF16)
    r.d_up[...] = (d_hidden * (gate_pre * sigma)).astype(BF16)
    spread(gm, wide, wide, mm(r.d_gate[...], normed_mid, NN))
    rs(GATE, 0)
    spread(gm, 2 * wide, wide, mm(r.d_up[...], normed_mid, NN))
    rs(UP, 0)
    r.part_m[:, :, 0:D] = (
        mm(r.hidden[...], wd[pl.ds(at_down, wide), :], TN).astype(BF16).reshape(4, length // 4, D)
    )
    r.part_m[:, :, D : 2 * D] = (
        (
            mm(r.d_gate[...], wd[pl.ds(at_gate, wide), :], TN)
            + mm(r.d_up[...], wd[pl.ds(at_up, wide), :], TN)
        )
        .astype(BF16)
        .reshape(4, length // 4, D)
    )
    sum_m[0]()
    rs(DOWN, 1)
    sum_m[1]()
    rs(GATE, 1)
    summed = sum_m[2]()
    resid_mid = r.resid_mid[...]
    r.v_resid[...] = resid_mid + summed[:, 0:D]
    emit(r.v_resid, r.resid_out)
    d_normmid = summed[:, D : 2 * D]
    inv_mlp = rms_scale(resid_mid)
    mlp_row = jnp.sum(d_normmid * resid_mid * inv_mlp, axis=0, keepdims=True)
    scaled = gain_mlp * d_normmid
    d_mid = (
        r.cot_in[...]
        + inv_mlp * scaled
        - resid_mid * inv_mlp**3 * jnp.mean(scaled * resid_mid, axis=-1, keepdims=True)
    )
    r.d_mid[...] = d_mid
    r.dmid4[me] = d_mid.astype(BF16)
    gather_d[0]()
    rs(UP, 1)
    rs(DOWN, 2)
    gather_d[1]()
    rs(GATE, 2)
    gather_d[2]()

    dmid_bf = r.dmid4[...].reshape(length, D)
    gated = r.gated[...]
    rs(UP, 2)
    d_gated = mm(dmid_bf, wd[pl.ds(at_out, DV), :], NT)
    spread(go, 0, DV, mm(gated, dmid_bf, TN))
    rs(OUT, 0)
    rs(DOWN, 3)
    outgate = proj[:, 2 * DK + DV : 2 * DK + 2 * DV]
    mixed = r.mixed[...]
    inv_head = rms_scale(mixed)
    sigma = jax.nn.sigmoid(outgate)
    d_head = d_gated * (outgate * sigma)
    r.d_proj[:, 2 * DK + DV : 2 * DK + 2 * DV] = (
        d_gated * (mixed * inv_head * gain_head) * sigma * (1.0 + outgate * (1.0 - sigma))
    ).astype(BF16)
    head_row = jnp.sum(d_head * mixed * inv_head, axis=0, keepdims=True)
    scaled = gain_head * d_head
    d_mixed = inv_head * scaled - mixed * inv_head**3 * jnp.mean(
        scaled * mixed, axis=-1, keepdims=True
    )
    query_dec, seg_l = r.query_dec[...], r.seg_l[...]
    prior = r.prior[0:1]
    last_seg = [seg_l[(c + 1) * GROUP - 1 : (c + 1) * GROUP] for c in range(groups)]
    before = [prior] + last_seg[:-1]
    grown = r.grown[...]
    dec = [
        grown[(c + 1) * GROUP - 1 : (c + 1) * GROUP] * (last_seg[c] == before[c]).astype(F32)
        for c in range(groups)
    ]
    rs(GATE, 3)
    pulls = []
    for c in range(groups):
        inherit = (group(seg_l, c) == before[c]).astype(F32)
        pulls.append(exact(group(d_mixed, c), inherit * group(query_dec, c), TN))
    total = pulls[groups - 1]
    through = dec[groups - 1]
    for c in range(groups - 2, -1, -1):
        total = pulls[c] + dec[c] * total
        through = through * dec[c]
    r.chain_send[1, pl.ds(0, DV)] = total.astype(BF16)
    r.chain_send[1, pl.ds(DV, 16)] = lines_of(through)
    chain_start(1)
    rs(UP, 3)
    rs(OUT, 1)
    value = proj[:, 2 * DK : 2 * DK + DV]
    key_inc = r.key_inc[...]
    ti = lax.broadcasted_iota(jnp.int32, (length, length), 0)
    tj = lax.broadcasted_iota(jnp.int32, (length, length), 1)
    below = jnp.logical_and(ti // GROUP == tj // GROUP, ti >= tj)
    seg_row = r.seg_in[...].astype(F32) + 1.0
    seg_wide = jnp.concatenate([seg_l] * (length // DK), axis=1)
    joined = jnp.logical_and(below, seg_wide == seg_row)
    d_scores = jnp.where(joined, exact(d_mixed, value, NT), 0.0)
    d_value = exact(r.scores[...], d_mixed, TN)
    rs(DOWN, 4)
    carried = jnp.concatenate(
        [
            (group(seg_l, c) == before[c]).astype(F32) * exact(group(d_mixed, c), r.states[c], NN)
            for c in range(groups)
        ],
        axis=0,
    )
    d_query_dec = exact(d_scores, key_inc, NN) + carried
    d_key_inc = exact(d_scores, query_dec, TN)
    rs(GATE, 4)
    rs(UP, 4)
    rs(OUT, 2)
    chain_wait(1)
    pull = chain_sum(1)
    key = proj[:, DK : 2 * DK]
    fade = r.fade[...]
    key_final = key * fade
    d_finals, d_values, d_ends = [None] * groups, [None] * groups, [None] * groups
    for c in range(groups - 1, -1, -1):
        d_final = exact(group(value, c), pull, NN)
        d_finals[c] = d_final
        d_values[c] = group(d_value, c) + exact(group(key_final, c), pull, NT)
        d_end = jnp.sum(d_final * group(key_final, c), axis=0, keepdims=True) + dec[c] * jnp.sum(
            r.states[c] * pull, axis=0, keepdims=True
        )
        d_ends[c] = jnp.broadcast_to(d_end, (GROUP, DK))
        pull = pulls[c] + dec[c] * pull
    rs(DOWN, 5)
    d_final = jnp.concatenate(d_finals, axis=0)
    r.d_proj[:, 0:DK] = (d_query_dec * grown * scale).astype(BF16)
    r.d_proj[:, DK : 2 * DK] = (d_key_inc * r.shrunk[...] + d_final * fade).astype(BF16)
    r.d_proj[:, 2 * DK : 2 * DK + DV] = jnp.concatenate(d_values, axis=0).astype(BF16)
    d_cumul = d_query_dec * query_dec - d_key_inc * key_inc - d_final * key_final
    above = jnp.logical_and(ti // GROUP == tj // GROUP, ti <= tj)
    d_logdec = exact(above.astype(F32), d_cumul, NN) + jnp.concatenate(d_ends, axis=0)
    logit = r.logit[...]
    d_logit = d_logdec * jax.nn.sigmoid(-logit) / 16.0
    bias_row = jnp.sum(d_logit, axis=0, keepdims=True)
    rank = folded(wd[pl.ds(16, 16), :].astype(F32))
    grad_rank = exact(r.low[...], d_logit, TN)
    d_low = exact(d_logit, rank, NT).astype(BF16)
    d_proj = r.d_proj[...]
    normed = r.normed[...]
    gp[...] = mm(normed, d_proj, TN).astype(BF16).reshape(gp.shape)
    rs(PROJ, 0)
    r.part_i[...] = (
        (mm(d_proj, wp[...], NT) + mm(d_low, wd[pl.ds(0, 16), :], NN))
        .astype(BF16)
        .reshape(r.part_i.shape)
    )
    sum_i[0]()
    rs(GATE, 5)
    rs(PROJ, 1)
    sum_i[1]()
    rs(UP, 5)
    rs(OUT, 3)
    low_rows = mm(d_low, normed, TN)
    rs(PROJ, 2)
    d_normin = sum_i[2]()
    resid_in = r.x_in[...]
    inv_attn = rms_scale(resid_in)
    attn_row = jnp.sum(d_normin * resid_in * inv_attn, axis=0, keepdims=True)
    scaled = gain_attn * d_normin
    r.v_in[...] = (
        r.d_mid[...]
        + inv_attn * scaled
        - resid_in * inv_attn**3 * jnp.mean(scaled * resid_in, axis=-1, keepdims=True)
    )
    emit(r.v_in, r.grad_in)
    gs = r.gs
    gs[...] = jnp.zeros_like(gs)
    for b in range(n):
        cut = slice(b * LANE, (b + 1) * LANE)
        gs[b, 0:16] = low_rows[:, cut]
        gs[b, 16:32] = grad_rank
        gs[b, 32:33] = attn_row[:, cut]
        gs[b, 33:34] = mlp_row[:, cut]
        gs[b, 34:35] = head_row[:, 0:LANE]
        gs[b, 35:36] = head_row[:, LANE : 2 * LANE]
        gs[b, 36:37] = bias_row
    lean = [
        remote(
            gs.at[(s + d) % n],
            r.gs_recv.at[d - 1],
            r.gs_ssem.at[d - 1],
            r.gs_rsem.at[d - 1],
            SHARD,
            (s + d) % n,
        )
        for d in range(1, n)
    ]
    for copy in lean:
        copy.start()
    rs(DOWN, 6)
    rs(PROJ, 3)
    rs(GATE, 6)
    rs(OUT, 4)
    mine = gs[s]
    for d, copy in enumerate(lean):
        copy.wait_recv()
        mine = mine + r.gs_recv[d]
    r.lean_send[...] = mine
    heads = [
        remote(
            r.lean_send,
            r.hs_recv.at[d - 1],
            r.hs_ssem.at[d - 1],
            r.hs_rsem.at[d - 1],
            HEAD,
            (me + d) % 4,
        )
        for d in range(1, 4)
    ]
    for copy in heads:
        copy.start()
    rs(PROJ, 4)
    rs(UP, 6)
    rs(OUT, 5)
    rs_finish(DOWN)
    rs(PROJ, 5)
    rs_finish(GATE)
    rs(OUT, 6)
    for d, copy in enumerate(heads):
        copy.wait_recv()
        mine = mine + r.hs_recv[d]
    quarter = LANE // 4
    by_head = pltpu.roll(mine, (LANE - quarter * me) % LANE, 1)
    by_shard = pltpu.roll(r.lean_send[...], (LANE - part_k * s) % LANE, 1)
    gains = pltpu.roll(mine, (2 * LANE - part_v * s - (part_v // 4) * me) % LANE, 1)
    r.lean[0:16] = by_head[0:16]
    r.lean[16:32] = by_shard[16:32]
    r.lean[32:48] = jnp.concatenate(
        [by_head[32:34], jnp.where(lower, gains[34:35], gains[35:36]), by_shard[36:37], by_head[36:48]],
        axis=0,
    )
    emit(r.lean, r.g_lean)
    rs(PROJ, 6)
    rs_finish(UP)
    rs_finish(OUT)
    rs_finish(PROJ)
    for copy in lean + heads:
        copy.wait_send()
    for one in (gather_x, gather_c, gather_m, gather_d, sum_o, sum_m, sum_i):
        one[3]()
    chain_drain(0)
    chain_drain(1)
    ag_drain()
    rs_drain()
    for copy in written:
        copy.wait()


def finish_kernel(count, *refs):
    ins, outs = refs[:count], refs[count + 1 : 2 * count + 1]
    lean = refs[count]
    small = refs[2 * count + 1 : 2 * count + 7]
    stage = refs[2 * count + 7 : 3 * count + 7]
    held, rank, low, attn, mlp, head, bias, in_sem, out_sem = refs[3 * count + 7 :]
    first = pltpu.make_async_copy(lean, held, in_sem.at[count])
    first.start()
    there = [pltpu.make_async_copy(a, b, in_sem.at[i]) for i, (a, b) in enumerate(zip(ins, stage))]
    for copy in there:
        copy.start()
    first.wait()
    for i in range(GATE_RANK):
        rank[i] = held[16 + i : 17 + i, 0 : rank.shape[2]]
    low[...] = held[0:16, 0 : low.shape[1]]
    attn[...] = held[32:33, 0 : attn.shape[1]]
    mlp[...] = held[33:34, 0 : mlp.shape[1]]
    head[...] = held[34:35, 0 : head.shape[1]]
    bias[...] = held[35:36, 0 : bias.shape[1]]
    back = [
        pltpu.make_async_copy(a, b, out_sem.at[i])
        for i, (a, b) in enumerate(
            zip(stage + (rank, low, attn, mlp, head, bias), outs + small)
        )
    ]
    for copy in back[count:]:
        copy.start()
    for one, copy in zip(there, back):
        one.wait()
        copy.start()
    for copy in back:
        copy.wait()


def finish(large, lean, n):
    count = len(large)
    shapes = ((GATE_RANK, 1, DK // n), (GATE_RANK, LANE // 4), (1, LANE // 4), (1, LANE // 4), (1, DV // n // 4), (1, DK // n))
    sem = pltpu.SemaphoreType.DMA
    made = pl.pallas_call(
        functools.partial(finish_kernel, count),
        out_shape=tuple(jax.ShapeDtypeStruct(a.shape, F32) for a in large)
        + tuple(jax.ShapeDtypeStruct(a, F32) for a in shapes),
        in_specs=[pl.BlockSpec(memory_space=pl.ANY)] * (count + 1),
        out_specs=tuple([pl.BlockSpec(memory_space=pl.ANY)] * (count + 6)),
        scratch_shapes=[pltpu.VMEM(a.shape, F32) for a in large]
        + [pltpu.VMEM((SMALL, LANE), F32)]
        + [pltpu.VMEM(a, F32) for a in shapes]
        + [sem((count + 1,)), sem((count + 6,))],
        compiler_params=pltpu.CompilerParams(vmem_limit_bytes=60 * 1024 * 1024),
    )(*large, lean)
    return made[:count], made[count:]


def block(args, ident):
    n = lax.axis_size(SHARD)
    ins = Refs(args)
    wide = ins.w_down.shape[0]
    rows = ins.resid_in.shape[0]
    length = ins.segment.shape[1]
    depth = ins.w_query.shape[0]
    groups = length // GROUP
    reach = min(n - 1, (SEQ + length - 2) // length)

    def out(*shape):
        return jax.ShapeDtypeStruct(shape, F32)

    outs = dict(
        resid_out=out(rows, D),
        grad_in=out(rows, D),
        g_query=out(depth, DK),
        g_key=out(depth, DK),
        g_value=out(depth, DV),
        g_outgate=out(depth, DV),
        g_out=out(DV, LANE),
        g_gate=out(wide, LANE),
        g_up=out(wide, LANE),
        g_down=out(wide, LANE),
        g_lean=out(SMALL, LANE),
    )
    across = 2 * DK + 2 * DV
    tall = SMALL + DV + 3 * wide
    vm = pltpu.VMEM
    sem = pltpu.SemaphoreType.DMA
    scratch = dict(
        wp=vm((D, across), BF16),
        wd=vm((tall, D), BF16),
        x4=vm((4, rows, D), F32),
        cot4=vm((4, rows, D), BF16),
        mid4=vm((4, rows, D), BF16),
        dmid4=vm((4, rows, D), BF16),
        normed=vm((length, D), BF16),
        proj=vm((length, across), F32),
        low=vm((length, GATE_RANK), F32),
        logit=vm((length, DK), F32),
        fade=vm((length, DK), F32),
        grown=vm((length, DK), F32),
        shrunk=vm((length, DK), F32),
        seg_l=vm((length, DK), F32),
        query_dec=vm((length, DK), F32),
        key_inc=vm((length, DK), F32),
        scores=vm((length, length), F32),
        mixed=vm((length, DV), F32),
        states=vm((groups, DV, DK), F32),
        prior=vm((8, DK), F32),
        x_in=vm((rows, D), F32),
        cot_in=vm((rows, D), F32),
        seg_in=vm((1, length), jnp.int32),
        s_low=vm((GATE_RANK, LANE), BF16),
        s_rank=vm((GATE_RANK, DK // n), BF16),
        s_attn=vm((1, LANE), BF16),
        s_mlp=vm((1, LANE), BF16),
        s_head=vm((1, DV // n), BF16),
        s_bias=vm((1, DK // n), BF16),
        pad=vm((32, LANE), F32),
        small=vm((SMALL, LANE), BF16),
        v_resid=vm((rows, D), F32),
        v_in=vm((rows, D), F32),
        v_proj=vm((depth, across), F32),
        v_out=vm((DV, LANE), F32),
        v_gate=vm((wide, LANE), F32),
        v_up=vm((wide, LANE), F32),
        v_down=vm((wide, LANE), F32),
        lean=vm((SMALL, LANE), F32),
        gated=vm((length, DV), BF16),
        resid_mid=vm((rows, D), F32),
        d_mid=vm((rows, D), F32),
        gate_pre=vm((wide, length), F32),
        up_pre=vm((wide, length), F32),
        hidden=vm((wide, length), BF16),
        d_gate=vm((wide, length), BF16),
        d_up=vm((wide, length), BF16),
        d_proj=vm((length, across), BF16),
        gm=vm((n, 3 * wide, LANE), BF16),
        go=vm((n, DV, LANE), BF16),
        gp=vm((n, depth, across), BF16),
        gs=vm((n, SMALL, LANE), F32),
        gs_recv=vm((n - 1, SMALL, LANE), F32),
        lean_send=vm((SMALL, LANE), F32),
        hs_recv=vm((3, SMALL, LANE), F32),
        held_m=vm((n - 1, 3 * wide, LANE), BF16),
        held_o=vm((n - 1, DV, LANE), BF16),
        held_p=vm((n - 1, depth, across), BF16),
        chain_send=vm((2, DV + 16, DK), BF16),
        chain_recv=vm((2, reach, DV + 16, DK), BF16),
    )
    for tag, width in (("o", D), ("m", 2 * D), ("i", D)):
        scratch["part_" + tag] = vm((4, rows, width), BF16)
        scratch["near_" + tag] = vm((2, rows, width), BF16)
        scratch["far_" + tag] = vm((rows, width), BF16)
        scratch["total_" + tag] = vm((rows, width), BF16)
    scratch.update(
        ag_send=sem((11, 2, n // 2)),
        ag_recv=sem((11, 2, n // 2)),
        rs_send=sem((12, n - 1)),
        rs_recv=sem((12, n - 1)),
        qg_send=sem((4, 2, 3)),
        qg_recv=sem((4, 2, 3)),
        qs_send=sem((3, 2, 3)),
        qs_recv=sem((3, 2, 3)),
        chain_ssem=sem((2, reach)),
        chain_rsem=sem((2, reach)),
        gs_ssem=sem((n - 1,)),
        gs_rsem=sem((n - 1,)),
        hs_ssem=sem((3,)),
        hs_rsem=sem((3,)),
        own_sem=sem((17,)),
        out_sem=sem((27,)),
    )
    names = tuple(ins) + tuple(outs) + tuple(scratch)
    made = pl.pallas_call(
        functools.partial(block_kernel, n, reach, names),
        out_shape=tuple(outs.values()),
        in_specs=[pl.BlockSpec(memory_space=pl.ANY)] * len(ins),
        out_specs=tuple(pl.BlockSpec(memory_space=pl.ANY) for _ in outs),
        scratch_shapes=list(scratch.values()),
        compiler_params=pltpu.CompilerParams(
            collective_id=ident, has_side_effects=True, vmem_limit_bytes=60 * 1024 * 1024
        ),
    )(*ins.values())
    return Refs(zip(outs, made))


def fused(
    resid_in,
    cotangent,
    segment,
    attn_gain,
    w_query,
    w_key,
    w_value,
    w_outgate,
    w_low,
    w_rank,
    rank_bias,
    head_gain,
    w_out,
    mlp_gain,
    w_gate,
    w_up,
    w_down,
):
    n = lax.axis_size(SHARD)
    got = block(
        dict(
            resid_in=resid_in,
            cotangent=cotangent,
            segment=segment.reshape(1, -1),
            w_query=w_query,
            w_key=w_key,
            w_value=w_value,
            w_outgate=w_outgate,
            w_low=w_low.T,
            w_rank=w_rank[:, 0, :],
            attn_gain=attn_gain.reshape(1, -1),
            mlp_gain=mlp_gain.reshape(1, -1),
            head_gain=head_gain.reshape(1, -1),
            rank_bias=rank_bias,
            w_out=w_out,
            w_gate=w_gate.T,
            w_up=w_up.T,
            w_down=w_down,
        ),
        1,
    )
    names = [k for k in got if k != "g_lean"]
    large, (rank, low, attn, mlp, head, bias) = finish([got[k] for k in names], got.g_lean, n)
    got = Refs(zip(names, large))
    return (
        got.resid_out,
        got.grad_in,
        attn.reshape(-1),
        got.g_query,
        got.g_key,
        got.g_value,
        got.g_outgate,
        low.T,
        rank,
        bias,
        head.reshape(-1),
        got.g_out,
        mlp.reshape(-1),
        got.g_gate.T,
        got.g_up.T,
        got.g_down,
    )


def on_device(*args):
    n = lax.axis_size(SHARD)
    rows = args[4].shape[0]
    if rows == LANE and n % 2 == 0 and lax.axis_size(HEAD) == 4 and DK % n == 0:
        return fused(*args)
    return split_up(*args)


def solution(mesh):
    in_specs = (
        P((SHARD, HEAD), None),
        P((SHARD, HEAD), None),
        P(SHARD),
        P(SHARD),
        P(SHARD, HEAD),
        P(SHARD, HEAD),
        P(SHARD, HEAD),
        P(SHARD, HEAD),
        P(SHARD, None),
        P(None, HEAD, SHARD),
        P(HEAD, SHARD),
        P(SHARD),
        P(HEAD, SHARD),
        P(SHARD),
        P(SHARD, HEAD),
        P(SHARD, HEAD),
        P(HEAD, SHARD),
    )
    out_specs = (
        P((SHARD, HEAD), None),
        P((SHARD, HEAD), None),
        P((SHARD, HEAD)),
        P(SHARD, HEAD),
        P(SHARD, HEAD),
        P(SHARD, HEAD),
        P(SHARD, HEAD),
        P((SHARD, HEAD), None),
        P(None, HEAD, SHARD),
        P(HEAD, SHARD),
        P((SHARD, HEAD)),
        P(HEAD, SHARD),
        P((SHARD, HEAD)),
        P(SHARD, HEAD),
        P(SHARD, HEAD),
        P(HEAD, SHARD),
    )
    return jax.shard_map(
        on_device, mesh=mesh, in_specs=in_specs, out_specs=out_specs, check_vma=False
    )
```
